128 devices in a mesh: mem: 8 (over x, core), tile: 16 (over y, z).
Axes of the slice: x: 4, y: 4, z: 4, core: 2. Of those that a mesh axis runs over, the one named last changes fastest.
Arguments:
- control: float32 [16, 64, 320, 160], P('mem', None, 'tile'), may hold values from -6 to 6
- ens_perts: float32 [16, 2, 64, 320, 160], P('mem', None, None, 'tile'), may hold values from -8 to 8
- vert_corr: float32 [64, 64], replicated, may hold values from -0.75 to 0.75
- slab_wts: float32 [16, 4], replicated, may hold values from 0.25 to 2
- level_slab: int32 [64], replicated, may hold values from 0 to 15, as said below
Outputs:
- wind_share: float32 [2, 64, 320, 160], P(None, 'mem', 'tile')
- gradient: float32 [16, 64, 320, 160], P('mem', None, 'tile')
The draws below stay inside these ranges and needn't reach their ends.
Inputs may be any that keep to these rules, and one draw needn't show every extreme that they name: `level_slab`: each slab holds a contiguous run of levels and slab numbers never fall with the level; every slab holds 1 to 8 levels, and one slab holds exactly 8.
All inputs are finite; a program needn't handle non-finite values.
Results may differ from the reference program's by a relative error of at most 0.0001.
Values sent between devices are 32-bit elements; how exact they have to be, the bound alone decides.
No kernel may reach another device: no remote copies, remote signals or barrier semaphores. Data moves between devices by JAX's collectives and lax.ppermute only.
A program may use at most 128 MiB of HBM per device.

```python
import math
import jax
import jax.numpy as jnp
from jax import lax

NX = 320
NY = 160
COMP = 2
L = 64
M = 16
SLABS = 16
CAP = 8


def draw_level_slab(key, part):
    key_pick, key_perm = jax.random.split(jax.random.fold_in(key, 17))
    full_slab = jax.random.randint(key_pick, (), 0, SLABS)
    extra = L - CAP - (SLABS - 1)
    candidates = (SLABS - 1) * (CAP - 1)
    order = jax.random.permutation(key_perm, candidates)
    chosen = (order < extra).astype(jnp.int32)
    owners = jnp.arange(candidates) // (CAP - 1)
    others = jnp.arange(SLABS - 1)
    extra_counts = jnp.sum((owners[None, :] == others[:, None]).astype(jnp.int32) * chosen[None, :], axis=1)
    actual = others + (others >= full_slab).astype(others.dtype)
    counts = jnp.zeros((SLABS,), jnp.int32).at[actual].set((1 + extra_counts).astype(jnp.int32))
    counts = counts.at[full_slab].set(CAP)
    ends = jnp.cumsum(counts)
    levels = jnp.arange(L)
    return jnp.sum((ends[None, :] <= levels[:, None]).astype(jnp.int32), axis=1).astype(jnp.int32)


def raised(result, own_key, source, target, blocks, factor):
    def block_of(dim):
        return (jnp.arange(result.shape[dim]) // (result.shape[dim] // blocks)).reshape((-1,) + (1,) * (result.ndim - 1 - dim))

    one_side = jax.random.permutation(own_key, blocks)[block_of(target)]
    second = (block_of(target) + blocks // 2) % blocks
    return jnp.where((block_of(source) == one_side) | (block_of(source) == second), factor * result, result)


def steps_of(rng, shape, cuts, low, top_value):
    def one(axis_at, shards_of):
        steps = jax.random.uniform(jax.random.fold_in(jax.random.fold_in(rng, 6), axis_at), (shards_of,), jnp.float32, low / len(cuts), top_value / len(cuts))
        return jnp.repeat(jnp.exp(steps), shape[axis_at] // shards_of).reshape((-1,) + (1,) * (len(shape) - axis_at - 1))

    level = one(*cuts[0])
    for cut in cuts[1:]:
        level = level * one(*cut)
    return level


def bell_draw(stream_key, extent, width, bound, shards=(), kind=jnp.bfloat16):
    loudness = steps_of(stream_key, extent, shards, -0.22, 0.18) if shards else 1.0
    result = jax.random.normal(stream_key, extent, jnp.float32) * width * loudness
    return jnp.minimum(jnp.maximum(result, -bound), bound).astype(kind)


def gaussian_with(rng, extent, deviation, reach, cuts, heavy, kind=jnp.bfloat16):
    drawn = deviation * jax.random.normal(rng, extent, jnp.float32)
    if cuts:
        drawn = drawn * steps_of(rng, extent, cuts, -0.22, 0.18)
    return jnp.clip(raised(drawn, jax.random.fold_in(rng, 3), *heavy), -reach, reach).astype(kind)


def setup_inputs(seed: int = 0) -> dict:
    key_list = jax.random.split(jax.random.key(seed), 6)
    return {
        "control": bell_draw(key_list[0], (M, L, NX, NY), 1.0, 6.0, ((0, 8), (2, 16)), jnp.float32),
        "ens_perts": gaussian_with(key_list[1], (M, COMP, L, NX, NY), 1.0, 8.0, ((0, 8), (3, 16)), (0, 2, 8, 2.0), jnp.float32),
        "vert_corr": bell_draw(key_list[2], (L, L), L ** -0.5, 0.75, (), jnp.float32),
        "slab_wts": jnp.clip(jnp.exp(jax.random.uniform(key_list[3], (SLABS, 4), jnp.float32, math.log(0.25), math.log(2.0))), 0.25, 2.0),
        "level_slab": draw_level_slab(jax.random.fold_in(key_list[5], 71), 0),
    }


dilation_steps = (1, 2, 4, 8)
highest = lax.Precision.HIGHEST

def line_filter(length, dilation):
    positions = jnp.arange(length)
    distance = jnp.abs(positions[None, :] - positions[:, None])
    inside = (distance % dilation == 0) & (distance <= 6 * dilation)
    ratio = (distance // dilation).astype(jnp.float32)
    kernel = jnp.where(inside, jnp.exp(-ratio * ratio / 8.0), 0.0).astype(jnp.float32)
    cubed = jnp.dot(jnp.dot(kernel, kernel, precision=highest), kernel, precision=highest)
    centre = cubed[:, length // 2]
    return cubed / jnp.sqrt(jnp.sum(centre * centre))

def horizontal(fields, weights, filters):
    running = jnp.zeros(fields.shape, jnp.float32)
    for scale_num in range(len(filters)):
        along_x, along_y = filters[scale_num]
        stepped = jnp.einsum('ij,...jy->...iy', along_x, fields, precision=highest)
        stepped = jnp.einsum('...iy,ly->...il', stepped, along_y, precision=highest)
        running = running + weights[:, scale_num][:, None, None] * stepped
    return running

def reference(control, ens_perts, vert_corr, slab_wts, level_slab):
    level_wts = slab_wts[level_slab]
    filters = [(line_filter(NX, dilation), line_filter(NY, dilation)) for dilation in dilation_steps]
    member_scale = 1.0 / math.sqrt(M - 1)

    def forward(level_field):
        smooth = horizontal(level_field, level_wts, filters)
        return jnp.einsum('lm,mxy->lxy', vert_corr, smooth, precision=highest)
    localized = lax.map(forward, control)
    wind_share = jnp.einsum('mclxy,mlxy->clxy', ens_perts, localized, precision=highest) * member_scale

    def backward(member_pert):
        adjoint = lax.optimization_barrier(jnp.sum(member_pert * wind_share, axis=0)) * member_scale
        adjoint = jnp.einsum('ml,mxy->lxy', vert_corr, adjoint, precision=highest)
        return horizontal(adjoint, level_wts, filters)
    gradient = control + lax.map(backward, ens_perts)
    return (wind_share, gradient)
```

```python
import math

import jax
import jax.numpy as jnp
import ml_dtypes
import numpy as np
from jax import lax
from jax.experimental import pallas as pl
from jax.experimental.pallas import tpu as pltpu
from jax.sharding import PartitionSpec as P

DILATIONS = (1, 2, 4, 8)
TILES = 16
MEMS = 8
ROWS = 20
NX = 320
NY = 160
LV = 64
MAIN = 128
TAIL = 32
GROUPS = ROWS // 4
K = ROWS + GROUPS
STEP = 5
FIELDS = 8
NS = len(DILATIONS)
YC = NS * NY
VMEM = 56 * 1024 * 1024
bf16 = jnp.bfloat16
f32 = jnp.float32


def line_filter(length, dilation):
    positions = np.arange(length)
    distance = np.abs(positions[None, :] - positions[:, None])
    inside = (distance % dilation == 0) & (distance <= 6 * dilation)
    ratio = (distance // dilation).astype(np.float64)
    kernel = np.where(inside, np.exp(-ratio * ratio / 8.0), 0.0)
    cubed = kernel @ kernel @ kernel
    centre = cubed[:, length // 2]
    return cubed / np.sqrt(np.sum(centre * centre))


def split_np(a):
    hi = a.astype(np.float32).astype(ml_dtypes.bfloat16)
    lo = (a - hi.astype(np.float64)).astype(np.float32).astype(ml_dtypes.bfloat16)
    return hi, lo


def x_order():
    order = []
    for j in range(4):
        for g in range(GROUPS):
            for t in range(TILES):
                order.append(ROWS * t + 4 * g + j)
    return np.array(order)


def constants():
    order = x_order()
    gx = np.concatenate(
        [line_filter(NX, d)[order][:, order] for d in DILATIONS], axis=1
    )
    gys = [line_filter(NY, d).T for d in DILATIONS]
    gy = np.concatenate([g[:, :MAIN] for g in gys] + [g[:, MAIN:] for g in gys], axis=1)
    return split_np(gx), split_np(gy)


def split(a):
    hi = a.astype(bf16)
    lo = (a - hi.astype(f32)).astype(bf16)
    return hi, lo


def dot(a, b):
    return jnp.dot(a, b, preferred_element_type=f32)


def params():
    return pltpu.CompilerParams(vmem_limit_bytes=VMEM)


def pack_body(x_ref, o_ref):
    for r in range(ROWS):
        o_ref[0, :, r] = x_ref[0, r, :, :MAIN].reshape(LV // 8, 8, MAIN)
    for g in range(GROUPS):
        tails = [x_ref[0, 4 * g + j, :, MAIN:] for j in range(4)]
        o_ref[0, :, ROWS + g] = jnp.concatenate(tails, axis=1).reshape(LV // 8, 8, MAIN)


def pack(x):
    n = x.shape[0]
    return pl.pallas_call(
        pack_body,
        grid=(n,),
        in_specs=[pl.BlockSpec((1, ROWS, LV, NY), lambda i: (i, 0, 0, 0))],
        out_specs=pl.BlockSpec((1, LV // 8, K, 8, MAIN), lambda i: (i, 0, 0, 0, 0)),
        out_shape=jax.ShapeDtypeStruct((n, LV // 8, K, 8, MAIN), f32),
        compiler_params=params(),
        name="pack",
    )(x)


def finish_body(y_ref, c_ref, o_ref):
    for r in range(ROWS):
        o_ref[0, r, :, :MAIN] = c_ref[0, r, :, :MAIN] + y_ref[0, :, r].reshape(LV, MAIN)
    for g in range(GROUPS):
        tails = y_ref[0, :, ROWS + g].reshape(LV, MAIN)
        for j in range(4):
            r = 4 * g + j
            o_ref[0, r, :, MAIN:] = c_ref[0, r, :, MAIN:] + tails[:, TAIL * j : TAIL * (j + 1)]


def finish(y, control):
    n = y.shape[0]
    natural = pl.BlockSpec((1, ROWS, LV, NY), lambda i: (i, 0, 0, 0))
    return pl.pallas_call(
        finish_body,
        grid=(n,),
        in_specs=[pl.BlockSpec((1, LV // 8, K, 8, MAIN), lambda i: (i, 0, 0, 0, 0)), natural],
        out_specs=natural,
        out_shape=jax.ShapeDtypeStruct((n, ROWS, LV, NY), f32),
        compiler_params=params(),
        name="finish",
    )(y, control)


def field_rows(k, f):
    return pl.ds(8 * k + f, TILES, stride=8 * K)


def filter_body(x_ref, w_ref, gy_ref, gxs_ref, gxh_ref, o_ref, hi_ref, lo_ref):
    for j in range(4):
        parts = []
        for f in range(FIELDS):
            for g in range(GROUPS):
                pair = [x_ref[field_rows(k, f), :] for k in (4 * g + j, ROWS + g)]
                parts.append(jnp.concatenate(pair, axis=1))
        hi, lo = split(jnp.concatenate(parts, axis=0))
        y = dot(jnp.concatenate([hi, lo, hi], axis=1), gy_ref[j])
        span = TILES * GROUPS
        fields = [y[span * f : span * (f + 1)] * w_ref[f : f + 1, :] for f in range(FIELDS)]
        for s in range(NS):
            at = s * NX + j * span
            pieces = [fields[f][:, MAIN * s : MAIN * (s + 1)] for f in range(FIELDS)]
            for q in range(FIELDS // 4):
                lane = NS * MAIN + TAIL * s
                pieces.append(
                    jnp.concatenate(
                        [fields[4 * q + i][:, lane : lane + TAIL] for i in range(4)], axis=1
                    )
                )
            hi, lo = split(jnp.concatenate(pieces, axis=1))
            hi_ref[at : at + span, :] = hi
            lo_ref[at : at + span, :] = lo
    both = dot(gxs_ref[...], hi_ref[...])
    out = both[:NX] + both[NX:] + dot(gxh_ref[...], lo_ref[...])
    for f in range(FIELDS):
        for g in range(GROUPS):
            tails = []
            lane = FIELDS * MAIN + MAIN * (f // 4) + TAIL * (f % 4)
            for j in range(4):
                at = TILES * (GROUPS * j + g)
                o_ref[field_rows(4 * g + j, f), :] = out[
                    at : at + TILES, MAIN * f : MAIN * (f + 1)
                ]
                tails.append(out[at : at + TILES, lane : lane + TAIL])
            o_ref[field_rows(ROWS + g, f), :] = jnp.concatenate(tails, axis=1)


def filter_fields(x, w, gy, gxs, gxh):
    return pl.pallas_call(
        filter_body,
        out_shape=jax.ShapeDtypeStruct((TILES * K * FIELDS, MAIN), f32),
        scratch_shapes=[
            pltpu.VMEM((NS * NX, FIELDS * NY), bf16),
            pltpu.VMEM((NS * NX, FIELDS * NY), bf16),
        ],
        compiler_params=params(),
        name="filter",
    )(x, w, gy, gxs, gxh)


def mix(v_ref, x):
    hi, lo = split(x)
    vh, vl = split(v_ref[...])
    return dot(vh, hi) + dot(vh, lo) + dot(vl, hi)


def levels_at(ref, lead, at):
    tiles = [ref[lead + (slice(None), at + i)].reshape(LV, MAIN) for i in range(STEP)]
    return jnp.concatenate(tiles, axis=1)


def forward_body(x_ref, v_ref, e_ref, o_ref):
    for at in range(0, K, STEP):
        loc = [mix(v_ref, levels_at(x_ref, (m,), at)) for m in range(2)]
        for c in range(2):
            total = sum(levels_at(e_ref, (m, c), at) * loc[m] for m in range(2))
            for i in range(STEP):
                o_ref[:, c, at + i] = total[:, MAIN * i : MAIN * (i + 1)].reshape(MEMS, 8, MAIN)


def forward(x, v, ens):
    return pl.pallas_call(
        forward_body,
        out_shape=jax.ShapeDtypeStruct((MEMS, 2, K, 8, MAIN), f32),
        compiler_params=params(),
        name="forward",
    )(x, v, ens)


def total_body(scale, x_ref, o_ref, wind_ref):
    for c in range(2):
        total = x_ref[0, c]
        for k in range(1, MEMS):
            total = total + x_ref[k, c]
        total = total * scale
        for k in range(MEMS):
            o_ref[k, c] = total
        for r in range(ROWS):
            wind_ref[c, r, :, :MAIN] = total[r]
        for g in range(GROUPS):
            for j in range(4):
                wind_ref[c, 4 * g + j, :, MAIN:] = total[ROWS + g][:, TAIL * j : TAIL * (j + 1)]


def total(x, scale):
    return pl.pallas_call(
        lambda *refs: total_body(scale, *refs),
        out_shape=(
            jax.ShapeDtypeStruct((MEMS, 2, K, 8, MAIN), f32),
            jax.ShapeDtypeStruct((2, ROWS, LV // MEMS, NY), f32),
        ),
        compiler_params=params(),
        name="total",
    )(x)


def adjoint_body(scale, x_ref, v_ref, e_ref, o_ref):
    for at in range(0, K, STEP):
        wind = []
        for c in range(2):
            tiles = [x_ref[:, c, at + i].reshape(LV, MAIN) for i in range(STEP)]
            wind.append(jnp.concatenate(tiles, axis=1))
        for m in range(2):
            adj = sum(levels_at(e_ref, (m, c), at) * wind[c] for c in range(2)) * scale
            back = mix(v_ref, adj)
            for i in range(STEP):
                o_ref[m, :, at + i] = back[:, MAIN * i : MAIN * (i + 1)].reshape(LV // 8, 8, MAIN)


def adjoint(x, v, ens, scale):
    return pl.pallas_call(
        lambda *refs: adjoint_body(scale, *refs),
        out_shape=jax.ShapeDtypeStruct((2, LV // 8, K, 8, MAIN), f32),
        compiler_params=params(),
        name="adjoint",
    )(x, v, ens)


def tiles_swap(x):
    return lax.all_to_all(x.reshape(TILES, K, FIELDS, MAIN), "tile", 0, 0, tiled=True)


def shards(control, ens_perts, vert_corr, slab_wts, level_slab):
    members = control.shape[0]
    scale = 1.0 / math.sqrt(members * MEMS - 1)
    (gxh, gxl), (gyh, gyl) = constants()

    control = jnp.transpose(control, (0, 2, 1, 3))
    ens = jnp.transpose(ens_perts, (0, 1, 3, 2, 4)).reshape(4, ROWS, LV, NY)
    sent = pack(control)
    got = tiles_swap(sent)

    ens = pack(ens).reshape(2, 2, LV // 8, K, 8, MAIN)
    gxs = jnp.concatenate([jnp.asarray(gxh), jnp.asarray(gxl)], axis=0)
    variants = []
    for j in range(4):
        def wide(g):
            zeros = jnp.zeros((MAIN, YC), bf16)
            return jnp.concatenate([jnp.asarray(g[:MAIN]), zeros.at[TAIL * j : TAIL * (j + 1)].set(jnp.asarray(g[MAIN:]))], axis=0)
        high = wide(gyh)
        variants.append(jnp.concatenate([high, high, wide(gyl)], axis=0))
    gy = jnp.stack(variants)
    level_wts = slab_wts[level_slab]
    first = FIELDS * (lax.axis_index("tile") % (LV // FIELDS))
    own = lax.dynamic_slice_in_dim(level_wts, first, FIELDS, 0)
    w = jnp.concatenate([jnp.repeat(own, MAIN, axis=1), jnp.repeat(own, TAIL, axis=1)], axis=1)

    def smooth(x):
        return filter_fields(x.reshape(TILES * K * FIELDS, MAIN), w, gy, gxs, jnp.asarray(gxh))

    back = tiles_swap(smooth(got)).reshape(2, LV // 8, K, 8, MAIN)
    part = forward(back, vert_corr, ens)
    pieces = lax.all_to_all(part, "mem", 0, 0, tiled=True)
    copies, wind_share = total(pieces, scale)
    wind = lax.all_to_all(copies, "mem", 0, 0, tiled=True)
    adj = adjoint(wind, vert_corr.T, ens, scale)
    back = tiles_swap(smooth(tiles_swap(adj))).reshape(2, LV // 8, K, 8, MAIN)
    gradient = finish(back, control)
    return (jnp.transpose(wind_share, (0, 2, 1, 3)), jnp.transpose(gradient, (0, 2, 1, 3)))


def solution(mesh):
    return jax.shard_map(
        shards,
        mesh=mesh,
        in_specs=(P("mem", None, "tile", None), P("mem", None, None, "tile", None), P(), P(), P()),
        out_specs=(P(None, "mem", "tile", None), P("mem", None, "tile", None)),
        check_vma=False,
    )
```

```python
import math

import jax
import jax.numpy as jnp
import ml_dtypes
import numpy as np
from jax import lax
from jax.experimental import pallas as pl
from jax.experimental.pallas import tpu as pltpu
from jax.sharding import PartitionSpec as P


DILATIONS = (1, 2, 4, 8)
TILES = 16
MEMS = 8
ROWS = 20
NX = 320
NY = 160
LV = 64
MAIN = 128
TAIL = 32
GROUPS = ROWS // 4
K = ROWS + GROUPS
Q = 4
FIELDS = 8
NS = len(DILATIONS)
VMEM = 56 * 1024 * 1024
bf16 = jnp.bfloat16
f32 = jnp.float32


def line_filter(length, dilation):
    positions = np.arange(length)
    distance = np.abs(positions[None, :] - positions[:, None])
    inside = (distance % dilation == 0) & (distance <= 6 * dilation)
    ratio = (distance // dilation).astype(np.float64)
    kernel = np.where(inside, np.exp(-ratio * ratio / 8.0), 0.0)
    cubed = kernel @ kernel @ kernel
    centre = cubed[:, length // 2]
    return cubed / np.sqrt(np.sum(centre * centre))


def split_np(a):
    hi = a.astype(np.float32).astype(ml_dtypes.bfloat16)
    lo = (a - hi.astype(np.float64)).astype(np.float32).astype(ml_dtypes.bfloat16)
    return hi, lo


def x_order():
    order = []
    for j in range(4):
        for g in range(GROUPS):
            for t in range(TILES):
                order.append(ROWS * t + 4 * g + j)
    return np.array(order)


def constants():
    order = x_order()
    gx = np.concatenate(
        [line_filter(NX, d)[order][:, order] for d in DILATIONS], axis=1
    )
    gys = [line_filter(NY, d).T for d in DILATIONS]
    gy = np.concatenate([g[:, :MAIN] for g in gys] + [g[:, MAIN:] for g in gys], axis=1)
    gy = np.concatenate([gy, np.zeros((2 * MAIN - NY, NS * NY))], axis=0)
    return split_np(gx), split_np(gy)


def split(a):
    hi = a.astype(bf16)
    lo = (a - hi.astype(f32)).astype(bf16)
    return hi, lo


def dot(a, b):
    return jnp.dot(a, b, preferred_element_type=f32)


def params():
    return pltpu.CompilerParams(vmem_limit_bytes=VMEM)


def pack_body(x_ref, o_ref):
    for r in range(ROWS):
        o_ref[0, :, r] = x_ref[0, r, :, :MAIN].reshape(LV // 8, 8, MAIN)
    for g in range(GROUPS):
        tails = [x_ref[0, 4 * g + j, :, MAIN:] for j in range(4)]
        o_ref[0, :, ROWS + g] = jnp.concatenate(tails, axis=1).reshape(LV // 8, 8, MAIN)


def pack(x):
    n = x.shape[0]
    return pl.pallas_call(
        pack_body,
        grid=(n,),
        in_specs=[pl.BlockSpec((1, ROWS, LV, NY), lambda i: (i, 0, 0, 0))],
        out_specs=pl.BlockSpec((1, LV // 8, K, 8, MAIN), lambda i: (i, 0, 0, 0, 0)),
        out_shape=jax.ShapeDtypeStruct((n, LV // 8, K, 8, MAIN), f32),
        compiler_params=params(),
        name="pack",
    )(x)


def finish_body(y_ref, c_ref, o_ref):
    for r in range(ROWS):
        o_ref[0, r, :, :MAIN] = c_ref[0, r, :, :MAIN] + y_ref[0, :, r].reshape(LV, MAIN)
    for g in range(GROUPS):
        tails = y_ref[0, :, ROWS + g].reshape(LV, MAIN)
        for j in range(4):
            r = 4 * g + j
            o_ref[0, r, :, MAIN:] = c_ref[0, r, :, MAIN:] + tails[:, TAIL * j : TAIL * (j + 1)]


def finish(y, control):
    n = y.shape[0]
    natural = pl.BlockSpec((1, ROWS, LV, NY), lambda i: (i, 0, 0, 0))
    return pl.pallas_call(
        finish_body,
        grid=(n,),
        in_specs=[pl.BlockSpec((1, LV // 8, K, 8, MAIN), lambda i: (i, 0, 0, 0, 0)), natural],
        out_specs=natural,
        out_shape=jax.ShapeDtypeStruct((n, ROWS, LV, NY), f32),
        compiler_params=params(),
        name="finish",
    )(y, control)


def unpack_wind_body(x_ref, o_ref):
    for c in range(2):
        for r in range(ROWS):
            o_ref[c, r, :, :MAIN] = x_ref[r % MEMS, c, r // MEMS]
        for g in range(GROUPS):
            k = ROWS + g
            tails = x_ref[k % MEMS, c, k // MEMS]
            for j in range(4):
                o_ref[c, 4 * g + j, :, MAIN:] = tails[:, TAIL * j : TAIL * (j + 1)]


def unpack_wind(x):
    return pl.pallas_call(
        unpack_wind_body,
        out_shape=jax.ShapeDtypeStruct((2, ROWS, LV // MEMS, NY), f32),
        compiler_params=params(),
        name="unpack_wind",
    )(x)


def spread_body(me_ref, x_ref, *refs):
    o_refs, packed = refs[:MEMS], refs[MEMS]
    for r in range(ROWS):
        packed[r % MEMS, r // MEMS] = x_ref[0, r, :, :MAIN]
    for g in range(GROUPS):
        tails = [x_ref[0, 4 * g + j, :, MAIN:] for j in range(4)]
        k = ROWS + g
        packed[k % MEMS, k // MEMS] = jnp.concatenate(tails, axis=1)
    for k in range(K, MEMS * Q):
        packed[k % MEMS, k // MEMS] = jnp.zeros((LV, MAIN), f32)
    for k in range(MEMS):
        o_refs[k][0] = packed[lax.rem(me_ref[0] + k, MEMS)]


def spread(me, x):
    n = x.shape[0]
    return pl.pallas_call(
        spread_body,
        grid_spec=pltpu.PrefetchScalarGridSpec(
            num_scalar_prefetch=1,
            grid=(n,),
            in_specs=[pl.BlockSpec((1, ROWS, LV, NY), lambda i, me: (i, 0, 0, 0))],
            out_specs=[pl.BlockSpec((1, Q, LV, MAIN), lambda i, me: (i, 0, 0, 0))] * MEMS,
            scratch_shapes=[pltpu.VMEM((MEMS, Q, LV, MAIN), f32)],
        ),
        out_shape=[jax.ShapeDtypeStruct((n, Q, LV, MAIN), f32)] * MEMS,
        compiler_params=params(),
        name="spread",
    )(me, x)


def field_rows(k, f):
    return pl.ds(8 * k + f, TILES, stride=8 * K)


def share_rows(k, f):
    at = ((k % MEMS) * TILES * Q + k // MEMS) * 8 + f
    return pl.ds(at, TILES, stride=8 * Q)


def filter_body(in_rows, out_rows, x_ref, w_ref, gy_ref, gx_ref, o_ref, hi_ref, lo_ref):
    span = TILES * GROUPS
    for j in range(4):
        parts = []
        for f in range(FIELDS):
            for g in range(GROUPS):
                tail = x_ref[in_rows(ROWS + g, f), :]
                if j:
                    tail = pltpu.roll(tail, MAIN - TAIL * j, 1)
                main = x_ref[in_rows(4 * g + j, f), :]
                parts.append(jnp.concatenate([main, tail], axis=1))
        hi, lo = split(jnp.concatenate(parts, axis=0))
        y = dot(jnp.concatenate([hi, lo, hi], axis=1), gy_ref[...])
        fields = [y[span * f : span * (f + 1)] * w_ref[f : f + 1, :] for f in range(FIELDS)]
        for s in range(NS):
            at = s * NX + j * span
            pieces = [fields[f][:, MAIN * s : MAIN * (s + 1)] for f in range(FIELDS)]
            for q in range(FIELDS // 4):
                lane = NS * MAIN + TAIL * s
                pieces.append(
                    jnp.concatenate(
                        [fields[4 * q + i][:, lane : lane + TAIL] for i in range(4)], axis=1
                    )
                )
            hi, lo = split(jnp.concatenate(pieces, axis=1))
            hi_ref[at : at + span, :] = hi
            lo_ref[at : at + span, :] = lo
    both = dot(gx_ref[...], hi_ref[...])
    out = both[:NX] + both[NX:] + dot(gx_ref[:NX, :], lo_ref[...])
    for f in range(FIELDS):
        for g in range(GROUPS):
            tails = []
            lane = FIELDS * MAIN + MAIN * (f // 4) + TAIL * (f % 4)
            for j in range(4):
                at = TILES * (GROUPS * j + g)
                o_ref[out_rows(4 * g + j, f), :] = out[at : at + TILES, MAIN * f : MAIN * (f + 1)]
                tails.append(out[at : at + TILES, lane : lane + TAIL])
            o_ref[out_rows(ROWS + g, f), :] = jnp.concatenate(tails, axis=1)
    if out_rows is share_rows:
        for k in range(K, MEMS * Q):
            for f in range(FIELDS):
                o_ref[out_rows(k, f), :] = jnp.zeros((TILES, MAIN), f32)


def filter_fields(x, w, gy, gx, spread_out):
    rows = TILES * FIELDS * (MEMS * Q if spread_out else K)
    in_rows, out_rows = (field_rows, share_rows) if spread_out else (share_rows, field_rows)
    return pl.pallas_call(
        lambda *refs: filter_body(in_rows, out_rows, *refs),
        out_shape=jax.ShapeDtypeStruct((rows, MAIN), f32),
        scratch_shapes=[
            pltpu.VMEM((NS * NX, FIELDS * NY), bf16),
            pltpu.VMEM((NS * NX, FIELDS * NY), bf16),
        ],
        compiler_params=params(),
        name="filter_out" if spread_out else "filter_back",
    )(x, w, gy, gx)


def mix(v, x):
    hi, lo = split(x)
    return dot(v[0], hi) + dot(v[0], lo) + dot(v[1], hi)


def middle_body(scale, me_ref, x_ref, v_ref, vt_ref, *refs):
    e_refs, o_ref, wind_ref = refs[:MEMS], refs[MEMS], refs[MEMS + 1]
    v, vt = split(v_ref[...]), split(vt_ref[...])
    wind = [None, None]
    for k in range(MEMS):
        at = lax.rem(me_ref[0] + MEMS - k, MEMS)
        for m in range(2):
            tiles = [x_ref[at, m, :, q].reshape(LV, MAIN) for q in range(Q)]
            loc = mix(v, jnp.concatenate(tiles, axis=1))
            for c in range(2):
                ens = jnp.concatenate([e_refs[k][m, c, q] for q in range(Q)], axis=1)
                wind[c] = ens * loc if wind[c] is None else wind[c] + ens * loc
    wind = [w * scale for w in wind]
    for c in range(2):
        for q in range(Q):
            tile = wind[c][:, MAIN * q : MAIN * (q + 1)]
            wind_ref[:, c, q] = tile.reshape(MEMS, LV // MEMS, MAIN)
    for k in range(MEMS):
        at = lax.rem(me_ref[0] + MEMS - k, MEMS)
        for m in range(2):
            adj = None
            for c in range(2):
                ens = jnp.concatenate([e_refs[k][m, c, q] for q in range(Q)], axis=1)
                adj = ens * wind[c] if adj is None else adj + ens * wind[c]
            back = mix(vt, adj * scale)
            for q in range(Q):
                tile = back[:, MAIN * q : MAIN * (q + 1)]
                o_ref[at, m, :, q] = tile.reshape(LV // 8, 8, MAIN)


def middle(me, x, v, ens, scale):
    whole = pl.BlockSpec(memory_space=pltpu.VMEM)
    return pl.pallas_call(
        lambda *refs: middle_body(scale, *refs),
        in_specs=[pl.BlockSpec(memory_space=pltpu.SMEM)] + [whole] * (3 + MEMS),
        out_shape=(
            jax.ShapeDtypeStruct((MEMS, 2, LV // 8, Q, 8, MAIN), f32),
            jax.ShapeDtypeStruct((MEMS, 2, Q, LV // MEMS, MAIN), f32),
        ),
        compiler_params=params(),
        name="middle",
    )(me, x, v, v.T, *ens)


def swap(x, axes):
    return lax.all_to_all(x, axes, 0, 0, tiled=True)


def shards(control, ens_perts, vert_corr, slab_wts, level_slab):
    members = control.shape[0]
    scale = 1.0 / math.sqrt(members * MEMS - 1)
    (gxh, gxl), (gyh, gyl) = constants()

    control = jnp.transpose(control, (0, 2, 1, 3))
    got = swap(pack(control).reshape(TILES, K, FIELDS, MAIN), "tile")

    me = lax.axis_index("mem").reshape(1)
    ens = jnp.transpose(ens_perts, (0, 1, 3, 2, 4)).reshape(4, ROWS, LV, NY)
    ens = list(spread(me, ens))
    for k in range(1, MEMS):
        ens[k] = lax.ppermute(ens[k], "mem", [(i, (i + k) % MEMS) for i in range(MEMS)])
    ens = [e.reshape(2, 2, Q, LV, MAIN) for e in ens]

    gx = jnp.asarray(np.concatenate([gxh, gxl], axis=0))
    gy = jnp.asarray(np.concatenate([gyh, gyh, gyl], axis=0))
    level_wts = slab_wts[level_slab]
    first = FIELDS * (lax.axis_index("tile") % (LV // FIELDS))
    own = lax.dynamic_slice_in_dim(level_wts, first, FIELDS, 0)
    w = jnp.concatenate([jnp.repeat(own, MAIN, axis=1), jnp.repeat(own, TAIL, axis=1)], axis=1)

    smooth = filter_fields(got.reshape(TILES * K * FIELDS, MAIN), w, gy, gx, True)
    got = swap(smooth.reshape(MEMS * TILES, Q, FIELDS, MAIN), ("mem", "tile"))
    got = got.reshape(MEMS, 2, LV // 8, Q, 8, MAIN)
    adj, wind = middle(me, got, vert_corr, ens, scale)
    got = swap(adj.reshape(MEMS * TILES, Q, FIELDS, MAIN), ("mem", "tile"))
    got, wind = lax.optimization_barrier((got, wind))
    wind = unpack_wind(swap(wind, "mem"))
    smooth = filter_fields(got.reshape(MEMS * TILES * Q * FIELDS, MAIN), w, gy, gx, False)
    got = swap(smooth.reshape(TILES, K, FIELDS, MAIN), "tile")
    gradient = finish(got.reshape(2, LV // 8, K, 8, MAIN), control)
    return (jnp.transpose(wind, (0, 2, 1, 3)), jnp.transpose(gradient, (0, 2, 1, 3)))


def solution(mesh):
    return jax.shard_map(
        shards,
        mesh=mesh,
        in_specs=(P("mem", None, "tile", None), P("mem", None, None, "tile", None), P(), P(), P()),
        out_specs=(P(None, "mem", "tile", None), P("mem", None, "tile", None)),
        check_vma=False,
    )
```

```python
import math

import jax
import jax.numpy as jnp
import ml_dtypes
import numpy as np
from jax import lax
from jax.experimental import pallas as pl
from jax.experimental.pallas import tpu as pltpu
from jax.sharding import PartitionSpec as P


DILATIONS = (1, 2, 4, 8)
TILES = 16
MEMS = 8
ROWS = 20
NX = 320
NY = 160
LV = 64
MAIN = 128
TAIL = 32
GROUPS = ROWS // 4
K = ROWS + GROUPS
FULL = K // MEMS
Q = FULL + 1
LAST = K - 1
CUT = MAIN // MEMS
SHARE = FULL * LV + LV // MEMS
FIELDS = 8
NS = len(DILATIONS)
bf16 = jnp.bfloat16
f32 = jnp.float32


def line_filter(length, dilation):
    positions = np.arange(length)
    distance = np.abs(positions[None, :] - positions[:, None])
    inside = (distance % dilation == 0) & (distance <= 6 * dilation)
    ratio = (distance // dilation).astype(np.float64)
    kernel = np.where(inside, np.exp(-ratio * ratio / 8.0), 0.0)
    cubed = kernel @ kernel @ kernel
    centre = cubed[:, length // 2]
    return cubed / np.sqrt(np.sum(centre * centre))


def split_np(a):
    hi = a.astype(np.float32).astype(ml_dtypes.bfloat16)
    lo = (a - hi.astype(np.float64)).astype(np.float32).astype(ml_dtypes.bfloat16)
    return hi, lo


def x_order():
    order = []
    for j in range(4):
        for g in range(GROUPS):
            for t in range(TILES):
                order.append(ROWS * t + 4 * g + j)
    return np.array(order)


def constants():
    order = x_order()
    gx = np.concatenate(
        [line_filter(NX, d)[order][:, order] for d in DILATIONS], axis=1
    )
    gys = [line_filter(NY, d).T for d in DILATIONS]
    gy = np.concatenate([g[:, :MAIN] for g in gys] + [g[:, MAIN:] for g in gys], axis=1)
    gy = np.concatenate([gy, np.zeros((2 * MAIN - NY, NS * NY))], axis=0)
    return split_np(gx), split_np(gy)


def split(a):
    hi = a.astype(bf16)
    lo = (a - hi.astype(f32)).astype(bf16)
    return hi, lo


def dot(a, b):
    return jnp.dot(a, b, preferred_element_type=f32)


def params(mib):
    return pltpu.CompilerParams(vmem_limit_bytes=mib * 1024 * 1024)


WHOLE = pl.BlockSpec(memory_space=pltpu.VMEM)
HBM = pl.BlockSpec(memory_space=pltpu.HBM)
SMEM = pl.BlockSpec(memory_space=pltpu.SMEM)
dma = pltpu.SemaphoreType.DMA


def in_hbm(x):
    return pltpu.with_memory_space_constraint(x, pltpu.HBM)


def main_at(r):
    return 5 * (r // 4) + r % 4


def tail_at(g):
    return 5 * g + 4


def own_cut(i, shape):
    return lax.broadcasted_iota(jnp.int32, shape, len(shape) - 1) // CUT == i


def pack_body(x_hbm, o_hbm, x_ref, o_ref, in_sems, out_sems):
    blocks = [(m, g) for m in range(x_ref.shape[0]) for g in range(GROUPS)]
    loads, stores = [], []
    for n, (m, g) in enumerate(blocks):
        rows = pl.ds(4 * g, 4)
        loads.append(pltpu.make_async_copy(x_hbm.at[m, rows], x_ref.at[m, rows], in_sems.at[n]))
        loads[-1].start()
    for n, (m, g) in enumerate(blocks):
        loads[n].wait()
        for j in range(4):
            o_ref[m, :, 5 * g + j] = x_ref[m, 4 * g + j, :, :MAIN].reshape(LV // 8, 8, MAIN)
        tails = [x_ref[m, 4 * g + j, :, MAIN:] for j in range(4)]
        o_ref[m, :, 5 * g + 4] = jnp.concatenate(tails, axis=1).reshape(LV // 8, 8, MAIN)
        part = (m, slice(None), pl.ds(5 * g, 5))
        stores.append(pltpu.make_async_copy(o_ref.at[part], o_hbm.at[part], out_sems.at[n]))
        stores[-1].start()
    for copy in stores:
        copy.wait()


def pack(x):
    n = x.shape[0]
    shape = (n, LV // 8, K, 8, MAIN)
    return pl.pallas_call(
        pack_body,
        in_specs=[HBM],
        out_specs=HBM,
        out_shape=pltpu.HBM(shape, f32),
        scratch_shapes=[
            pltpu.VMEM((n, ROWS, LV, NY), f32),
            pltpu.VMEM(shape, f32),
            dma((n * GROUPS,)),
            dma((n * GROUPS,)),
        ],
        compiler_params=params(12),
        name="pack",
    )(in_hbm(x))


def finish_body(y_ref, c_ref, o_hbm, o_ref, sems):
    stores = []
    for m in range(o_ref.shape[0]):
        for g in range(GROUPS):
            tails = y_ref[m, :, 5 * g + 4].reshape(LV, MAIN)
            for j in range(4):
                r = 4 * g + j
                main = y_ref[m, :, 5 * g + j].reshape(LV, MAIN)
                o_ref[m, r, :, :MAIN] = c_ref[m, r, :, :MAIN] + main
                tail = tails[:, TAIL * j : TAIL * (j + 1)]
                o_ref[m, r, :, MAIN:] = c_ref[m, r, :, MAIN:] + tail
            part = (m, pl.ds(4 * g, 4))
            n = len(stores)
            stores.append(pltpu.make_async_copy(o_ref.at[part], o_hbm.at[part], sems.at[n]))
            stores[-1].start()
    for copy in stores:
        copy.wait()


def finish(y, control):
    n = y.shape[0]
    shape = (n, ROWS, LV, NY)
    return pl.pallas_call(
        finish_body,
        in_specs=[WHOLE, WHOLE],
        out_specs=HBM,
        out_shape=jax.ShapeDtypeStruct(shape, f32),
        scratch_shapes=[pltpu.VMEM(shape, f32), dma((n * GROUPS,))],
        compiler_params=params(12),
        name="finish",
    )(y, control)


def unpack_wind_body(me_ref, *refs):
    got_refs, o_ref, x_ref = refs[:MEMS], refs[MEMS], refs[MEMS + 1]
    for k in range(MEMS):
        x_ref[lax.rem(me_ref[0] + MEMS - k, MEMS)] = got_refs[k][...]
    for c in range(2):
        last = x_ref[0, c, FULL]
        for i in range(1, MEMS):
            last = jnp.where(own_cut(i, last.shape), x_ref[i, c, FULL], last)
        for r in range(ROWS):
            k = main_at(r)
            o_ref[c, r, :, :MAIN] = x_ref[k % MEMS, c, k // MEMS]
        for g in range(GROUPS):
            k = tail_at(g)
            tails = last if k == LAST else x_ref[k % MEMS, c, k // MEMS]
            for j in range(4):
                o_ref[c, 4 * g + j, :, MAIN:] = tails[:, TAIL * j : TAIL * (j + 1)]


def unpack_wind(me, got):
    return pl.pallas_call(
        unpack_wind_body,
        in_specs=[SMEM] + [WHOLE] * MEMS,
        out_shape=jax.ShapeDtypeStruct((2, ROWS, LV // MEMS, NY), f32),
        scratch_shapes=[pltpu.VMEM((MEMS, 2, Q, LV // MEMS, MAIN), f32)],
        compiler_params=params(8),
        name="unpack_wind",
    )(me, *got)


def spread_body(me_ref, x_ref, *refs):
    o_refs, packed = refs[:MEMS], refs[MEMS]

    def keep(k, value):
        packed[k % MEMS, LV * (k // MEMS) : LV * (k // MEMS + 1)] = value

    for r in range(ROWS):
        keep(main_at(r), x_ref[0, r, :, :MAIN])
    for g in range(GROUPS):
        tails = jnp.concatenate([x_ref[0, 4 * g + j, :, MAIN:] for j in range(4)], axis=1)
        if tail_at(g) != LAST:
            keep(tail_at(g), tails)
    tiles = [tails[8 * u : 8 * (u + 1)] for u in range(LV // 8)]
    for d in range(MEMS):
        joined = pltpu.roll(tiles[0], CUT * (-d % MEMS), 1) if d else tiles[0]
        for u in range(1, LV // 8):
            shift = (u - d) % MEMS
            moved = pltpu.roll(tiles[u], CUT * shift, 1) if shift else tiles[u]
            joined = jnp.where(own_cut(u, joined.shape), moved, joined)
        packed[d, FULL * LV :] = joined
    for k in range(MEMS):
        o_refs[k][0] = packed[lax.rem(me_ref[0] + k, MEMS)]


def spread(me, x):
    n = x.shape[0]
    return pl.pallas_call(
        spread_body,
        grid_spec=pltpu.PrefetchScalarGridSpec(
            num_scalar_prefetch=1,
            grid=(n,),
            in_specs=[pl.BlockSpec((1, ROWS, LV, NY), lambda i, me: (i, 0, 0, 0))],
            out_specs=[pl.BlockSpec((1, SHARE, MAIN), lambda i, me: (i, 0, 0))] * MEMS,
            scratch_shapes=[pltpu.VMEM((MEMS, SHARE, MAIN), f32)],
        ),
        out_shape=[pltpu.HBM((n, SHARE, MAIN), f32)] * MEMS,
        compiler_params=params(12),
        name="spread",
    )(me, in_hbm(x))


def field_rows(k, f):
    return pl.ds(8 * k + f, TILES, stride=8 * K)


def share_rows(i, q, f):
    return pl.ds((i * TILES * Q + q) * 8 + f, TILES, stride=8 * Q)


def load_tile(ref, shared, k, f):
    if not shared:
        return ref[field_rows(k, f), :]
    if k != LAST:
        return ref[share_rows(k % MEMS, k // MEMS, f), :]
    value = ref[share_rows(0, FULL, f), :]
    for i in range(1, MEMS):
        value = jnp.where(own_cut(i, value.shape), ref[share_rows(i, FULL, f), :], value)
    return value


def store_tile(ref, shared, k, f, value):
    if not shared:
        ref[field_rows(k, f), :] = value
    elif k != LAST:
        ref[share_rows(k % MEMS, k // MEMS, f), :] = value
    else:
        for i in range(MEMS):
            ref[share_rows(i, FULL, f), :] = value


def filter_body(
    out_shared, x_ref, w_ref, gy_hbm, gx_hbm, o_hbm, lhs_ref, gy_ref, gx_ref, hi_ref, lo_ref, o_ref, sems
):
    wide = 2 * MAIN
    parts = ((0, 0), (0, wide), (wide, 2 * wide))
    copies = [
        pltpu.make_async_copy(gy_hbm.at[pl.ds(a, wide)], gy_ref.at[pl.ds(b, wide)], sems.at[n])
        for n, (a, b) in enumerate(parts)
    ]
    copies.append(pltpu.make_async_copy(gx_hbm, gx_ref, sems.at[3]))
    for copy in copies:
        copy.start()
    span = TILES * GROUPS
    count = span * FIELDS

    def put(j, f, g, at, value):
        hi, lo = split(value)
        rows = slice(count * j + span * f + TILES * g, count * j + span * f + TILES * (g + 1))
        lhs_ref[rows, at : at + MAIN] = hi
        lhs_ref[rows, wide + at : wide + at + MAIN] = lo
        lhs_ref[rows, 2 * wide + at : 2 * wide + at + MAIN] = hi

    for f in range(FIELDS):
        for g in range(GROUPS):
            tail = load_tile(x_ref, not out_shared, tail_at(g), f)
            for j in range(4):
                moved = pltpu.roll(tail, MAIN - TAIL * j, 1) if j else tail
                put(j, f, g, MAIN, moved)
                put(j, f, g, 0, load_tile(x_ref, not out_shared, main_at(4 * g + j), f))
    for copy in copies[:3]:
        copy.wait()
    for j in range(4):
        y = dot(lhs_ref[count * j : count * (j + 1), :], gy_ref[...])
        fields = [y[span * f : span * (f + 1)] * w_ref[f : f + 1, :] for f in range(FIELDS)]
        for s in range(NS):
            at = s * NX + j * span
            pieces = [fields[f][:, MAIN * s : MAIN * (s + 1)] for f in range(FIELDS)]
            for q in range(FIELDS // 4):
                lane = NS * MAIN + TAIL * s
                pieces.append(
                    jnp.concatenate(
                        [fields[4 * q + i][:, lane : lane + TAIL] for i in range(4)], axis=1
                    )
                )
            hi, lo = split(jnp.concatenate(pieces, axis=1))
            hi_ref[at : at + span, :] = hi
            lo_ref[at : at + span, :] = lo
    copies[3].wait()
    both = dot(gx_ref[...], hi_ref[...])
    out = both[:NX] + both[NX:] + dot(gx_ref[:NX, :], lo_ref[...])

    def result(k, f):
        g, j = k // 5, k % 5
        at = [TILES * (GROUPS * i + g) for i in range(4)]
        if j < 4:
            return out[at[j] : at[j] + TILES, MAIN * f : MAIN * (f + 1)]
        lane = FIELDS * MAIN + MAIN * (f // 4) + TAIL * (f % 4)
        return jnp.concatenate([out[a : a + TILES, lane : lane + TAIL] for a in at], axis=1)

    if out_shared:
        rows = TILES * Q * FIELDS
        batches = [[LAST]] + [[i + MEMS * q for q in range(FULL)] for i in range(MEMS)]
    else:
        batches = [[5 * g + j for j in range(5)] for g in range(GROUPS)]
    stores = []
    for n, batch in enumerate(batches):
        for k in batch:
            for f in range(FIELDS):
                store_tile(o_ref, out_shared, k, f, result(k, f))
        sem = sems.at[4 + len(stores)]
        if out_shared and n:
            part = pl.ds(rows * (n - 1), rows)
            stores.append(pltpu.make_async_copy(o_ref.at[part], o_hbm.at[part], sem))
            stores[-1].start()
        elif not out_shared and n == len(batches) - 1:
            stores.append(pltpu.make_async_copy(o_ref, o_hbm, sem))
            stores[-1].start()
    for copy in stores:
        copy.wait()


def filter_fields(x, w, gy, gx, out_shared):
    rows = TILES * FIELDS * (MEMS * Q if out_shared else K)
    return pl.pallas_call(
        lambda *refs: filter_body(out_shared, *refs),
        in_specs=[WHOLE, WHOLE, HBM, HBM],
        out_specs=HBM,
        out_shape=pltpu.HBM((rows, MAIN), f32),
        scratch_shapes=[
            pltpu.VMEM((FIELDS * NX, 6 * MAIN), bf16),
            pltpu.VMEM((6 * MAIN, NS * NY), bf16),
            pltpu.VMEM((2 * NX, NS * NX), bf16),
            pltpu.VMEM((NS * NX, FIELDS * NY), bf16),
            pltpu.VMEM((NS * NX, FIELDS * NY), bf16),
            pltpu.VMEM((rows, MAIN), f32),
            dma((4 + MEMS,)),
        ],
        compiler_params=params(36),
        name="filter_out" if out_shared else "filter_back",
    )(x, w, in_hbm(gy), in_hbm(gx))


def mix(v, x):
    hi, lo = split(x)
    return dot(v[0], hi) + dot(v[0], lo) + dot(v[1], hi)


def middle_body(scale, me_ref, x_ref, v_ref, vt_ref, *refs):
    e_refs, o_ref, wind_refs = refs[:MEMS], refs[MEMS], refs[MEMS + 1 : 2 * MEMS + 1]
    cut_ref, wind_ref = refs[2 * MEMS + 1 :]
    v, vt = split(v_ref[...]), split(vt_ref[...])
    me = me_ref[0]
    wind = [None, None]
    for k in range(MEMS):
        at = lax.rem(me + MEMS - k, MEMS)
        for m in range(2):
            tiles = [x_ref[at, m, :, q].reshape(LV, MAIN) for q in range(Q)]
            loc = mix(v, jnp.concatenate(tiles, axis=1))
            for c in range(2):
                joined = e_refs[k][m, c, FULL * LV :]
                for u in range(LV // 8):
                    moved = pltpu.roll(joined, CUT * lax.rem(me + MEMS - u, MEMS), 1)
                    cut_ref[k, m, c, 8 * u : 8 * (u + 1)] = moved
                tiles = [e_refs[k][m, c, LV * q : LV * (q + 1)] for q in range(FULL)]
                ens = jnp.concatenate(tiles + [cut_ref[k, m, c]], axis=1)
                wind[c] = ens * loc if wind[c] is None else wind[c] + ens * loc
    wind = [w * scale for w in wind]
    for c in range(2):
        for q in range(Q):
            tile = wind[c][:, MAIN * q : MAIN * (q + 1)]
            wind_ref[:, c, q] = tile.reshape(MEMS, LV // MEMS, MAIN)
    for k in range(MEMS):
        wind_refs[k][...] = wind_ref[lax.rem(me + k, MEMS)]
    for k in range(MEMS):
        at = lax.rem(me + MEMS - k, MEMS)
        for m in range(2):
            adj = None
            for c in range(2):
                tiles = [e_refs[k][m, c, LV * q : LV * (q + 1)] for q in range(FULL)]
                ens = jnp.concatenate(tiles + [cut_ref[k, m, c]], axis=1)
                adj = ens * wind[c] if adj is None else adj + ens * wind[c]
            back = mix(vt, adj * scale)
            for q in range(Q):
                tile = back[:, MAIN * q : MAIN * (q + 1)]
                o_ref[at, m, :, q] = tile.reshape(LV // 8, 8, MAIN)


def middle(me, x, v, ens, scale):
    return pl.pallas_call(
        lambda *refs: middle_body(scale, *refs),
        in_specs=[SMEM] + [WHOLE] * (3 + MEMS),
        out_specs=[WHOLE] * (1 + MEMS),
        out_shape=[jax.ShapeDtypeStruct((MEMS, 2, LV // 8, Q, 8, MAIN), f32)]
        + [jax.ShapeDtypeStruct((2, Q, LV // MEMS, MAIN), f32)] * MEMS,
        scratch_shapes=[
            pltpu.VMEM((MEMS, 2, 2, LV, MAIN), f32),
            pltpu.VMEM((MEMS, 2, Q, LV // MEMS, MAIN), f32),
        ],
        compiler_params=params(24),
        name="middle",
    )(me, x, v, v.T, *ens)


def swap(x, axes):
    return lax.all_to_all(x, axes, 0, 0, tiled=True)


def shards(control, ens_perts, vert_corr, slab_wts, level_slab):
    members = control.shape[0]
    scale = 1.0 / math.sqrt(members * MEMS - 1)
    (gxh, gxl), (gyh, gyl) = constants()

    control = jnp.transpose(control, (0, 2, 1, 3))
    got = swap(pack(control).reshape(TILES, K, FIELDS, MAIN), "tile")

    me = lax.axis_index("mem").reshape(1)
    ens = jnp.transpose(ens_perts, (0, 1, 3, 2, 4)).reshape(4, ROWS, LV, NY)
    ens = list(spread(me, ens))
    for k in range(1, MEMS):
        ens[k] = lax.ppermute(ens[k], "mem", [(i, (i + k) % MEMS) for i in range(MEMS)])
    ens = [e.reshape(2, 2, SHARE, MAIN) for e in ens]

    gx = jnp.asarray(np.concatenate([gxh, gxl], axis=0))
    gy = jnp.asarray(np.concatenate([gyh, gyl], axis=0))
    level_wts = slab_wts[level_slab]
    first = FIELDS * (lax.axis_index("tile") % (LV // FIELDS))
    own = lax.dynamic_slice_in_dim(level_wts, first, FIELDS, 0)
    w = jnp.concatenate([jnp.repeat(own, MAIN, axis=1), jnp.repeat(own, TAIL, axis=1)], axis=1)

    smooth = filter_fields(got.reshape(TILES * K * FIELDS, MAIN), w, gy, gx, True)
    got = swap(smooth.reshape(MEMS * TILES, Q, FIELDS, MAIN), ("mem", "tile"))
    got = got.reshape(MEMS, 2, LV // 8, Q, 8, MAIN)
    adj, *wind = middle(me, got, vert_corr, ens, scale)
    got = swap(adj.reshape(MEMS * TILES, Q, FIELDS, MAIN), ("mem", "tile"))
    smooth = filter_fields(got.reshape(MEMS * TILES * Q * FIELDS, MAIN), w, gy, gx, False)
    smooth, wind = lax.optimization_barrier((smooth, wind))
    got = swap(smooth.reshape(TILES, K, FIELDS, MAIN), "tile")
    for k in range(1, MEMS):
        wind[k] = lax.ppermute(wind[k], "mem", [(i, (i + k) % MEMS) for i in range(MEMS)])
    wind = unpack_wind(me, wind)
    gradient = finish(got.reshape(2, LV // 8, K, 8, MAIN), control)
    return (jnp.transpose(wind, (0, 2, 1, 3)), jnp.transpose(gradient, (0, 2, 1, 3)))


def solution(mesh):
    return jax.shard_map(
        shards,
        mesh=mesh,
        in_specs=(P("mem", None, "tile", None), P("mem", None, None, "tile", None), P(), P(), P()),
        out_specs=(P(None, "mem", "tile", None), P("mem", None, "tile", None)),
        check_vma=False,
    )
```

```python
import math

import jax
import jax.numpy as jnp
import ml_dtypes
import numpy as np
from jax import lax
from jax.experimental import pallas as pl
from jax.experimental.pallas import tpu as pltpu
from jax.sharding import PartitionSpec as P


DILATIONS = (1, 2, 4, 8)
TILES = 16
MEMS = 8
ROWS = 20
NX = 320
NY = 160
LV = 64
MAIN = 128
TAIL = 32
GROUPS = ROWS // 4
K = ROWS + GROUPS
FULL = K // MEMS
Q = FULL + 1
LAST = K - 1
CUT = MAIN // MEMS
SHARE = FULL * LV + LV // MEMS
FIELDS = 8
NS = len(DILATIONS)
bf16 = jnp.bfloat16
f32 = jnp.float32


def line_filter(length, dilation):
    positions = np.arange(length)
    distance = np.abs(positions[None, :] - positions[:, None])
    inside = (distance % dilation == 0) & (distance <= 6 * dilation)
    ratio = (distance // dilation).astype(np.float64)
    kernel = np.where(inside, np.exp(-ratio * ratio / 8.0), 0.0)
    cubed = kernel @ kernel @ kernel
    centre = cubed[:, length // 2]
    return cubed / np.sqrt(np.sum(centre * centre))


def split_np(a):
    hi = a.astype(np.float32).astype(ml_dtypes.bfloat16)
    lo = (a - hi.astype(np.float64)).astype(np.float32).astype(ml_dtypes.bfloat16)
    return hi, lo


def x_order():
    order = []
    for j in range(4):
        for g in range(GROUPS):
            for t in range(TILES):
                order.append(ROWS * t + 4 * g + j)
    return np.array(order)


SPAN = TILES * GROUPS
FIRST = 2 * MAIN
REST = NX - FIRST
PAIR = REST + 2 * SPAN


def residue(j):
    return slice(SPAN * j, SPAN * (j + 1))


def constants():
    order = x_order()
    gx = [line_filter(NX, d)[order][:, order] for d in DILATIONS]
    gys = [line_filter(NY, d).T for d in DILATIONS]
    gy = np.concatenate([g[:, :MAIN] for g in gys] + [g[:, MAIN:] for g in gys], axis=1)
    high, low = split_np(gy)
    mains = NS * MAIN
    gy = np.concatenate([high, low[:, mains:], low[:, :mains]], axis=1)
    pairs, singles = [], []
    for p in range(2):
        rows = np.concatenate([np.arange(NX)[residue(p)], np.arange(NX)[residue(p + 2)]])
        pairs.append(np.concatenate([gx[0][rows, FIRST:], gx[1][rows][:, rows]], axis=1))
    for j in range(4):
        singles.append(np.concatenate([g[residue(j), residue(j)] for g in gx[2:]], axis=1))

    def stacked(a, axis):
        return jnp.asarray(np.concatenate(split_np(a), axis=axis))

    return (
        jnp.asarray(gy),
        stacked(gx[0][:, :FIRST], 0),
        stacked(np.stack(pairs), 1),
        stacked(np.stack(singles), 1),
    )


def split(a):
    hi = a.astype(bf16)
    lo = (a - hi.astype(f32)).astype(bf16)
    return hi, lo


def dot(a, b):
    return jnp.dot(a, b, preferred_element_type=f32)


def params(mib):
    return pltpu.CompilerParams(vmem_limit_bytes=mib * 1024 * 1024)


WHOLE = pl.BlockSpec(memory_space=pltpu.VMEM)
HBM = pl.BlockSpec(memory_space=pltpu.HBM)
SMEM = pl.BlockSpec(memory_space=pltpu.SMEM)
dma = pltpu.SemaphoreType.DMA


def in_hbm(x):
    return pltpu.with_memory_space_constraint(x, pltpu.HBM)


def main_at(r):
    return 5 * (r // 4) + r % 4


def tail_at(g):
    return 5 * g + 4


def own_cut(i, shape):
    return lax.broadcasted_iota(jnp.int32, shape, len(shape) - 1) // CUT == i


def pack_body(x_hbm, o_hbm, x_ref, o_ref, in_sems, out_sems):
    blocks = [(m, g) for m in range(x_ref.shape[0]) for g in range(GROUPS)]
    loads, stores = [], []
    for n, (m, g) in enumerate(blocks):
        rows = pl.ds(4 * g, 4)
        loads.append(pltpu.make_async_copy(x_hbm.at[m, rows], x_ref.at[m, rows], in_sems.at[n]))
        loads[-1].start()
    for n, (m, g) in enumerate(blocks):
        loads[n].wait()
        for j in range(4):
            o_ref[m, :, 5 * g + j] = x_ref[m, 4 * g + j, :, :MAIN].reshape(LV // 8, 8, MAIN)
        tails = [x_ref[m, 4 * g + j, :, MAIN:] for j in range(4)]
        o_ref[m, :, 5 * g + 4] = jnp.concatenate(tails, axis=1).reshape(LV // 8, 8, MAIN)
        part = (m, slice(None), pl.ds(5 * g, 5))
        stores.append(pltpu.make_async_copy(o_ref.at[part], o_hbm.at[part], out_sems.at[n]))
        stores[-1].start()
    for copy in stores:
        copy.wait()


def pack(x):
    n = x.shape[0]
    shape = (n, LV // 8, K, 8, MAIN)
    return pl.pallas_call(
        pack_body,
        in_specs=[HBM],
        out_specs=HBM,
        out_shape=pltpu.HBM(shape, f32),
        scratch_shapes=[
            pltpu.VMEM((n, ROWS, LV, NY), f32),
            pltpu.VMEM(shape, f32),
            dma((n * GROUPS,)),
            dma((n * GROUPS,)),
        ],
        compiler_params=params(12),
        name="pack",
    )(in_hbm(x))


def finish_body(y_hbm, c_ref, o_hbm, y_ref, o_ref, in_sems, sems):
    loads, stores = [], []
    for m in range(o_ref.shape[0]):
        for g in range(GROUPS):
            part = (m, slice(None), pl.ds(5 * g, 5))
            n = len(loads)
            loads.append(pltpu.make_async_copy(y_hbm.at[part], y_ref.at[part], in_sems.at[n]))
            loads[-1].start()
    for m in range(o_ref.shape[0]):
        for g in range(GROUPS):
            loads[len(stores)].wait()
            tails = y_ref[m, :, 5 * g + 4].reshape(LV, MAIN)
            for j in range(4):
                r = 4 * g + j
                main = y_ref[m, :, 5 * g + j].reshape(LV, MAIN)
                o_ref[m, r, :, :MAIN] = c_ref[m, r, :, :MAIN] + main
                tail = tails[:, TAIL * j : TAIL * (j + 1)]
                o_ref[m, r, :, MAIN:] = c_ref[m, r, :, MAIN:] + tail
            part = (m, pl.ds(4 * g, 4))
            n = len(stores)
            stores.append(pltpu.make_async_copy(o_ref.at[part], o_hbm.at[part], sems.at[n]))
            stores[-1].start()
    for copy in stores:
        copy.wait()


def finish(y, control):
    n = y.shape[0]
    shape = (n, ROWS, LV, NY)
    return pl.pallas_call(
        finish_body,
        in_specs=[HBM, WHOLE],
        out_specs=HBM,
        out_shape=pltpu.HBM(shape, f32),
        scratch_shapes=[
            pltpu.VMEM(y.shape, f32),
            pltpu.VMEM(shape, f32),
            dma((n * GROUPS,)),
            dma((n * GROUPS,)),
        ],
        compiler_params=params(16),
        name="finish",
    )(in_hbm(y), control)


def unpack_wind_body(me_ref, *refs):
    got_refs, o_ref, x_ref = refs[:MEMS], refs[MEMS], refs[MEMS + 1]
    for k in range(MEMS):
        x_ref[lax.rem(me_ref[0] + MEMS - k, MEMS)] = got_refs[k][...]
    for c in range(2):
        last = x_ref[0, c, FULL]
        for i in range(1, MEMS):
            last = jnp.where(own_cut(i, last.shape), x_ref[i, c, FULL], last)
        for r in range(ROWS):
            k = main_at(r)
            o_ref[c, r, :, :MAIN] = x_ref[k % MEMS, c, k // MEMS]
        for g in range(GROUPS):
            k = tail_at(g)
            tails = last if k == LAST else x_ref[k % MEMS, c, k // MEMS]
            for j in range(4):
                o_ref[c, 4 * g + j, :, MAIN:] = tails[:, TAIL * j : TAIL * (j + 1)]


def unpack_wind(me, got):
    return pl.pallas_call(
        unpack_wind_body,
        in_specs=[SMEM] + [WHOLE] * MEMS,
        out_shape=jax.ShapeDtypeStruct((2, ROWS, LV // MEMS, NY), f32),
        scratch_shapes=[pltpu.VMEM((MEMS, 2, Q, LV // MEMS, MAIN), f32)],
        compiler_params=params(8),
        name="unpack_wind",
    )(me, *got)


def spread_body(me_ref, x_hbm, *refs):
    o_refs, (x_ref, packed, in_sems, out_sems) = refs[:MEMS], refs[MEMS:]
    count = x_ref.shape[0]
    loads = [pltpu.make_async_copy(x_hbm.at[n], x_ref.at[n], in_sems.at[n]) for n in range(count)]
    for copy in loads:
        copy.start()
    stores = []
    for n in range(count):
        loads[n].wait()

        def keep(k, value):
            packed[n, k % MEMS, LV * (k // MEMS) : LV * (k // MEMS + 1)] = value

        for r in range(ROWS):
            keep(main_at(r), x_ref[n, r, :, :MAIN])
        for g in range(GROUPS):
            tails = jnp.concatenate([x_ref[n, 4 * g + j, :, MAIN:] for j in range(4)], axis=1)
            if tail_at(g) != LAST:
                keep(tail_at(g), tails)
        tiles = [tails[8 * u : 8 * (u + 1)] for u in range(LV // 8)]
        for d in range(MEMS):
            joined = pltpu.roll(tiles[0], CUT * (-d % MEMS), 1) if d else tiles[0]
            for u in range(1, LV // 8):
                shift = (u - d) % MEMS
                moved = pltpu.roll(tiles[u], CUT * shift, 1) if shift else tiles[u]
                joined = jnp.where(own_cut(u, joined.shape), moved, joined)
            packed[n, d, FULL * LV :] = joined
        for k in range(MEMS):
            share = packed.at[n, lax.rem(me_ref[0] + k, MEMS)]
            stores.append(pltpu.make_async_copy(share, o_refs[k].at[n], out_sems.at[n, k]))
            stores[-1].start()
    for copy in stores:
        copy.wait()


def spread(me, x):
    n = x.shape[0]
    return pl.pallas_call(
        spread_body,
        in_specs=[SMEM, HBM],
        out_specs=[HBM] * MEMS,
        out_shape=[pltpu.HBM((n, SHARE, MAIN), f32)] * MEMS,
        scratch_shapes=[
            pltpu.VMEM(x.shape, f32),
            pltpu.VMEM((n, MEMS, SHARE, MAIN), f32),
            dma((n,)),
            dma((n, MEMS)),
        ],
        compiler_params=params(16),
        name="spread",
    )(me, in_hbm(x))


def field_rows(k, f):
    return pl.ds(8 * k + f, TILES, stride=8 * K)


def share_rows(i, q, f):
    return pl.ds((i * TILES * Q + q) * 8 + f, TILES, stride=8 * Q)


def load_tile(ref, shared, k, f):
    if not shared:
        return ref[field_rows(k, f), :]
    if k != LAST:
        return ref[share_rows(k % MEMS, k // MEMS, f), :]
    value = ref[share_rows(0, FULL, f), :]
    for i in range(1, MEMS):
        value = jnp.where(own_cut(i, value.shape), ref[share_rows(i, FULL, f), :], value)
    return value


def filter_body(
    out_shared, x_ref, w_ref, gy_ref, ga_ref, gb_ref, gc_ref, o_hbm, ra_ref, rb_ref, rc_ref, last_ref, tails_ref, s_ref, o_ref, sems,
):
    wide = 2 * MAIN
    for f in range(FIELDS):
        last_ref[f] = load_tile(x_ref, not out_shared, LAST, f)

    def keep(s, j, lanes, value):
        for n, part in enumerate(split(value)):
            if s == 0:
                first = min(SPAN * (j + 1), FIRST) - SPAN * j
                ra_ref[n, SPAN * j : SPAN * j + first, lanes] = part[:first]
                if first < SPAN:
                    rb_ref[n, 0, :REST, lanes] = part[first:]
                    rb_ref[n, 1, :REST, lanes] = part[first:]
            elif s == 1:
                at = REST + SPAN * (j // 2)
                rb_ref[n, j % 2, at : at + SPAN, lanes] = part
            else:
                rc_ref[n, j, residue(s - 2), lanes] = part

    def y_filter(pair):
        parts = []
        for f in pair:
            for j in range(4):
                for g in range(GROUPS):
                    k = tail_at(g)
                    tail = last_ref[f] if k == LAST else load_tile(x_ref, not out_shared, k, f)
                    if j:
                        tail = pltpu.roll(tail, MAIN - TAIL * j, 1)
                    tail = tail[:, :TAIL]
                    main = load_tile(x_ref, not out_shared, main_at(4 * g + j), f)
                    parts.append(jnp.concatenate([main, tail], axis=1))
        hi, lo = split(jnp.concatenate(parts, axis=0))
        rows, cols = hi.shape[0], NS * NY
        both = dot(jnp.concatenate([hi, lo], axis=0), gy_ref[:, : cols + MAIN])
        y = both[:rows, :cols] + both[rows:, :cols]
        other = dot(hi, gy_ref[:, cols + MAIN :])
        y = y + jnp.concatenate([other, both[:rows, cols:]], axis=1)
        for i, f in enumerate(pair):
            lanes = slice(MAIN * f, MAIN * (f + 1))
            for j in range(4):
                at = SPAN * (4 * i + j)
                part = y[at : at + SPAN] * w_ref[f : f + 1, :]
                for s in range(NS):
                    keep(s, j, lanes, part[:, MAIN * s : MAIN * (s + 1)])
                tails_ref[f, j] = part[:, NS * MAIN :]

    def keep_tails():
        for q in range(FIELDS // 4):
            lanes = slice(MAIN * (FIELDS + q), MAIN * (FIELDS + q + 1))
            for j in range(4):
                for s in range(NS):
                    lane = TAIL * s
                    parts = [tails_ref[4 * q + i, j, :, lane : lane + TAIL] for i in range(4)]
                    keep(s, j, lanes, jnp.concatenate(parts, axis=1))

    def x_filter(lanes):
        def product(g, hi, lo):
            rows = g.shape[0] // 2
            both = dot(g, hi)
            return both[:rows] + both[rows:] + dot(g[:rows], lo)

        a = product(ga_ref[...], ra_ref[0, :, lanes], ra_ref[1, :, lanes])
        b = [product(gb_ref[p], rb_ref[0, p, :, lanes], rb_ref[1, p, :, lanes]) for p in range(2)]
        c = [product(gc_ref[j], rc_ref[0, j, :, lanes], rc_ref[1, j, :, lanes]) for j in range(4)]
        return [a[residue(j)] + b[j % 2][residue(j // 2)] + c[j] for j in range(4)]

    def x_main(pair):
        out = x_filter(slice(MAIN * pair[0], MAIN * pair[0] + wide))
        for i, f in enumerate(pair):
            for r in range(ROWS):
                g, j = r // 4, r % 4
                main = out[j][TILES * g : TILES * (g + 1), MAIN * i : MAIN * (i + 1)]
                at = TILES * (K * f + main_at(r))
                s_ref[at : at + TILES, :] = main

    def x_tails():
        out = x_filter(slice(MAIN * FIELDS, MAIN * FIELDS + wide))
        for f in range(FIELDS):
            lane = TAIL * f
            for g in range(GROUPS):
                rows = slice(TILES * g, TILES * (g + 1))
                parts = [out[j][rows, lane : lane + TAIL] for j in range(4)]
                at = TILES * (K * f + tail_at(g))
                s_ref[at : at + TILES, :] = jnp.concatenate(parts, axis=1)

    couples = [(f, f + 1) for f in range(0, FIELDS, 2)]
    y_filter(couples[0])
    y_filter(couples[1])
    x_main(couples[0])
    y_filter(couples[2])
    x_main(couples[1])
    y_filter(couples[3])
    keep_tails()
    x_main(couples[2])
    x_tails()
    x_main(couples[3])
    size = o_ref.shape[0] // MEMS
    stores = []
    for n in range(MEMS):
        if out_shared:
            cells = [(t, k, q) for q, k in enumerate([n, n + MEMS, n + 2 * MEMS, LAST]) for t in range(TILES)]
            spots = [(n * TILES + t) * Q + q for t, _, q in cells]
        else:
            cells = [(t, k, 0) for t in (2 * n, 2 * n + 1) for k in range(K)]
            spots = [K * t + k for t, k, _ in cells]
        for (t, k, _), at in zip(cells, spots):
            tile = s_ref[pl.ds(TILES * k + t, FIELDS, stride=TILES * K), :]
            o_ref[8 * at : 8 * (at + 1), :] = tile
        part = pl.ds(size * n, size)
        stores.append(pltpu.make_async_copy(o_ref.at[part], o_hbm.at[part], sems.at[n]))
        stores[-1].start()
    for copy in stores:
        copy.wait()


def filter_fields(x, w, filters, out_shared):
    rows = TILES * FIELDS * (MEMS * Q if out_shared else K)
    columns = FIELDS * NY
    return pl.pallas_call(
        lambda *refs: filter_body(out_shared, *refs),
        in_specs=[WHOLE] * (2 + len(filters)),
        out_specs=HBM,
        out_shape=pltpu.HBM((rows, MAIN), f32),
        scratch_shapes=[
            pltpu.VMEM((2, FIRST, columns), bf16),
            pltpu.VMEM((2, 2, PAIR, columns), bf16),
            pltpu.VMEM((2, 4, 2 * SPAN, columns), bf16),
            pltpu.VMEM((FIELDS, TILES, MAIN), f32),
            pltpu.VMEM((FIELDS, 4, SPAN, MAIN), f32),
            pltpu.VMEM((FIELDS * K * TILES, MAIN), f32),
            pltpu.VMEM((rows, MAIN), f32),
            dma((MEMS,)),
        ],
        compiler_params=params(36),
        name="filter_out" if out_shared else "filter_back",
    )(x, w, *filters)


def mix(v, x):
    hi, lo = split(x)
    return dot(v[0], hi) + dot(v[0], lo) + dot(v[1], hi)


def middle_body(scale, me_ref, x_ref, v_ref, *refs):
    e_refs, o_ref, wind_refs = list(refs[:MEMS]), refs[MEMS], refs[MEMS + 1 : 2 * MEMS + 1]
    cut_ref, wind_ref, ens_ref, sems = refs[2 * MEMS + 1 :]
    loads = [pltpu.make_async_copy(e_refs[k], ens_ref.at[k], sems.at[k]) for k in range(MEMS)]
    for copy in loads:
        copy.start()
    e_refs = [ens_ref.at[k] for k in range(MEMS)]
    v, vt = split(v_ref[...]), split(v_ref[...].T)
    me = me_ref[0]
    wind = [None, None]
    for k in range(MEMS):
        loads[k].wait()
        at = lax.rem(me + MEMS - k, MEMS)
        for m in range(2):
            tiles = [x_ref[at, m, :, q].reshape(LV, MAIN) for q in range(Q)]
            loc = mix(v, jnp.concatenate(tiles, axis=1))
            for c in range(2):
                joined = e_refs[k][m, c, FULL * LV :]
                for u in range(LV // 8):
                    moved = pltpu.roll(joined, CUT * lax.rem(me + MEMS - u, MEMS), 1)
                    cut_ref[k, m, c, 8 * u : 8 * (u + 1)] = moved
                tiles = [e_refs[k][m, c, LV * q : LV * (q + 1)] for q in range(FULL)]
                ens = jnp.concatenate(tiles + [cut_ref[k, m, c]], axis=1)
                wind[c] = ens * loc if wind[c] is None else wind[c] + ens * loc
    wind = [w * scale for w in wind]
    for c in range(2):
        for q in range(Q):
            tile = wind[c][:, MAIN * q : MAIN * (q + 1)]
            wind_ref[:, c, q] = tile.reshape(MEMS, LV // MEMS, MAIN)
    for k in range(MEMS):
        wind_refs[k][...] = wind_ref[lax.rem(me + k, MEMS)]
    for k in range(MEMS):
        at = lax.rem(me + MEMS - k, MEMS)
        for m in range(2):
            adj = None
            for c in range(2):
                tiles = [e_refs[k][m, c, LV * q : LV * (q + 1)] for q in range(FULL)]
                ens = jnp.concatenate(tiles + [cut_ref[k, m, c]], axis=1)
                adj = ens * wind[c] if adj is None else adj + ens * wind[c]
            back = mix(vt, adj * scale)
            for q in range(Q):
                tile = back[:, MAIN * q : MAIN * (q + 1)]
                o_ref[at, m, :, q] = tile.reshape(LV // 8, 8, MAIN)


def middle(me, x, v, ens, scale):
    return pl.pallas_call(
        lambda *refs: middle_body(scale, *refs),
        in_specs=[SMEM, WHOLE, WHOLE] + [HBM] * MEMS,
        out_specs=[WHOLE] * (1 + MEMS),
        out_shape=[jax.ShapeDtypeStruct((MEMS, 2, LV // 8, Q, 8, MAIN), f32)]
        + [jax.ShapeDtypeStruct((2, Q, LV // MEMS, MAIN), f32)] * MEMS,
        scratch_shapes=[
            pltpu.VMEM((MEMS, 2, 2, LV, MAIN), f32),
            pltpu.VMEM((MEMS, 2, Q, LV // MEMS, MAIN), f32),
            pltpu.VMEM((MEMS,) + ens[0].shape, f32),
            dma((MEMS,)),
        ],
        compiler_params=params(24),
        name="middle",
    )(me, x, v, *[in_hbm(e) for e in ens])


def swap(x, axes):
    return lax.all_to_all(x, axes, 0, 0, tiled=True)


ORDER = (2, 6, 4, 3, 5, 1, 7)


def shards(control, ens_perts, vert_corr, slab_wts, level_slab):
    members = control.shape[0]
    scale = 1.0 / math.sqrt(members * MEMS - 1)
    filters = constants()

    control = jnp.transpose(control, (0, 2, 1, 3))
    got = swap(pack(control).reshape(TILES, K, FIELDS, MAIN), "tile")

    me = lax.axis_index("mem").reshape(1)
    ens = jnp.transpose(ens_perts, (0, 1, 3, 2, 4)).reshape(4, ROWS, LV, NY)
    ens = list(spread(me, ens))
    for k in ORDER:
        ens[k] = lax.ppermute(ens[k], "mem", [(i, (i + k) % MEMS) for i in range(MEMS)])
    ens = [e.reshape(2, 2, SHARE, MAIN) for e in ens]

    level_wts = slab_wts[level_slab]
    first = FIELDS * (lax.axis_index("tile") % (LV // FIELDS))
    own = lax.dynamic_slice_in_dim(level_wts, first, FIELDS, 0)
    w = jnp.concatenate([jnp.repeat(own, MAIN, axis=1), jnp.repeat(own, TAIL, axis=1)], axis=1)

    smooth = filter_fields(got.reshape(TILES * K * FIELDS, MAIN), w, filters, True)
    got = swap(smooth.reshape(MEMS * TILES, Q, FIELDS, MAIN), ("mem", "tile"))
    got = got.reshape(MEMS, 2, LV // 8, Q, 8, MAIN)
    adj, *wind = middle(me, got, vert_corr, ens, scale)
    got = swap(adj.reshape(MEMS * TILES, Q, FIELDS, MAIN), ("mem", "tile"))
    smooth = filter_fields(got.reshape(MEMS * TILES * Q * FIELDS, MAIN), w, filters, False)
    smooth, wind = lax.optimization_barrier((smooth, wind))
    got = swap(smooth.reshape(TILES, K, FIELDS, MAIN), "tile")
    for k in range(1, MEMS):
        wind[k] = lax.ppermute(wind[k], "mem", [(i, (i + k) % MEMS) for i in range(MEMS)])
    wind = unpack_wind(me, wind)
    gradient = finish(got.reshape(2, LV // 8, K, 8, MAIN), control)
    return (jnp.transpose(wind, (0, 2, 1, 3)), jnp.transpose(gradient, (0, 2, 1, 3)))


def solution(mesh):
    return jax.shard_map(
        shards,
        mesh=mesh,
        in_specs=(P("mem", None, "tile", None), P("mem", None, None, "tile", None), P(), P(), P()),
        out_specs=(P(None, "mem", "tile", None), P("mem", None, "tile", None)),
        check_vma=False,
    )
```

```python
import math

import jax
import jax.numpy as jnp
import ml_dtypes
import numpy as np
from jax import lax
from jax.experimental import pallas as pl
from jax.experimental.pallas import tpu as pltpu
from jax.sharding import PartitionSpec as P


DILATIONS = (1, 2, 4, 8)
TILES = 16
MEMS = 8
ROWS = 20
NX = 320
NY = 160
LV = 64
MAIN = 128
TAIL = 32
GROUPS = ROWS // 4
K = ROWS + GROUPS
FULL = K // MEMS
Q = FULL + 1
LAST = K - 1
CUT = MAIN // MEMS
SHARE = FULL * LV + LV // MEMS
FIELDS = 8
NS = len(DILATIONS)
bf16 = jnp.bfloat16
f32 = jnp.float32


def line_filter(length, dilation):
    positions = np.arange(length)
    distance = np.abs(positions[None, :] - positions[:, None])
    inside = (distance % dilation == 0) & (distance <= 6 * dilation)
    ratio = (distance // dilation).astype(np.float64)
    kernel = np.where(inside, np.exp(-ratio * ratio / 8.0), 0.0)
    cubed = kernel @ kernel @ kernel
    centre = cubed[:, length // 2]
    return cubed / np.sqrt(np.sum(centre * centre))


def split_np(a):
    hi = a.astype(np.float32).astype(ml_dtypes.bfloat16)
    lo = (a - hi.astype(np.float64)).astype(np.float32).astype(ml_dtypes.bfloat16)
    return hi, lo


def x_order():
    order = []
    for j in range(4):
        for g in range(GROUPS):
            for t in range(TILES):
                order.append(ROWS * t + 4 * g + j)
    return np.array(order)


SPAN = TILES * GROUPS
FIRST = 2 * MAIN
REST = NX - FIRST
PAIR = REST + 2 * SPAN


def residue(j):
    return slice(SPAN * j, SPAN * (j + 1))


def constants():
    order = x_order()
    gx = [line_filter(NX, d)[order][:, order] for d in DILATIONS]
    gys = [line_filter(NY, d).T for d in DILATIONS]
    gy = np.concatenate([g[:, :MAIN] for g in gys] + [g[:, MAIN:] for g in gys], axis=1)
    high, low = split_np(gy)
    mains = NS * MAIN
    gy = np.concatenate([high, low[:, mains:], low[:, :mains]], axis=1)
    pairs, singles = [], []
    for p in range(2):
        rows = np.concatenate([np.arange(NX)[residue(p)], np.arange(NX)[residue(p + 2)]])
        pairs.append(np.concatenate([gx[0][rows, FIRST:], gx[1][rows][:, rows]], axis=1))
    for j in range(4):
        singles.append(np.concatenate([g[residue(j), residue(j)] for g in gx[2:]], axis=1))

    def stacked(a, axis):
        return jnp.asarray(np.concatenate(split_np(a), axis=axis))

    return (
        jnp.asarray(gy),
        stacked(gx[0][:, :FIRST], 0),
        stacked(np.stack(pairs), 1),
        stacked(np.stack(singles), 1),
    )


def split(a):
    hi = a.astype(bf16)
    lo = (a - hi.astype(f32)).astype(bf16)
    return hi, lo


def dot(a, b):
    return jnp.dot(a, b, preferred_element_type=f32)


def params(mib):
    return pltpu.CompilerParams(vmem_limit_bytes=mib * 1024 * 1024)


WHOLE = pl.BlockSpec(memory_space=pltpu.VMEM)
HBM = pl.BlockSpec(memory_space=pltpu.HBM)
SMEM = pl.BlockSpec(memory_space=pltpu.SMEM)
dma = pltpu.SemaphoreType.DMA


def in_hbm(x):
    return pltpu.with_memory_space_constraint(x, pltpu.HBM)


def main_at(r):
    return 5 * (r // 4) + r % 4


def tail_at(g):
    return 5 * g + 4


def gather_row(tile, shift):
    moved = pltpu.roll(pltpu.roll(tile, shift, 1), 0, 1, stride=CUT, stride_axis=0)
    here = lax.broadcasted_iota(jnp.int32, tile.shape, 0)
    lane = lax.broadcasted_iota(jnp.int32, tile.shape, 1) // CUT
    return jnp.sum(jnp.where(lane == here, moved, 0.0), axis=0, keepdims=True)


def own_cut(i, shape):
    return lax.broadcasted_iota(jnp.int32, shape, len(shape) - 1) // CUT == i


def pack_body(x_hbm, o_hbm, x_ref, o_ref, in_sems, out_sems):
    blocks = [(m, g) for m in range(x_ref.shape[0]) for g in range(GROUPS)]
    loads, stores = [], []
    for n, (m, g) in enumerate(blocks):
        rows = pl.ds(4 * g, 4)
        loads.append(pltpu.make_async_copy(x_hbm.at[m, rows], x_ref.at[m, rows], in_sems.at[n]))
        loads[-1].start()
    for n, (m, g) in enumerate(blocks):
        loads[n].wait()
        for j in range(4):
            o_ref[m, :, 5 * g + j] = x_ref[m, 4 * g + j, :, :MAIN].reshape(LV // 8, 8, MAIN)
        tails = [x_ref[m, 4 * g + j, :, MAIN:] for j in range(4)]
        o_ref[m, :, 5 * g + 4] = jnp.concatenate(tails, axis=1).reshape(LV // 8, 8, MAIN)
        part = (m, slice(None), pl.ds(5 * g, 5))
        stores.append(pltpu.make_async_copy(o_ref.at[part], o_hbm.at[part], out_sems.at[n]))
        stores[-1].start()
    for copy in stores:
        copy.wait()


def pack(x):
    n = x.shape[0]
    shape = (n, LV // 8, K, 8, MAIN)
    return pl.pallas_call(
        pack_body,
        in_specs=[HBM],
        out_specs=HBM,
        out_shape=pltpu.HBM(shape, f32),
        scratch_shapes=[
            pltpu.VMEM((n, ROWS, LV, NY), f32),
            pltpu.VMEM(shape, f32),
            dma((n * GROUPS,)),
            dma((n * GROUPS,)),
        ],
        compiler_params=params(12),
        name="pack",
    )(in_hbm(x))


def finish_body(y_hbm, c_ref, o_hbm, y_ref, o_ref, in_sems, sems):
    loads, stores = [], []
    for m in range(o_ref.shape[0]):
        for g in range(GROUPS):
            part = (m, slice(None), pl.ds(5 * g, 5))
            n = len(loads)
            loads.append(pltpu.make_async_copy(y_hbm.at[part], y_ref.at[part], in_sems.at[n]))
            loads[-1].start()
    for m in range(o_ref.shape[0]):
        for g in range(GROUPS):
            loads[len(stores)].wait()
            tails = y_ref[m, :, 5 * g + 4].reshape(LV, MAIN)
            for j in range(4):
                r = 4 * g + j
                main = y_ref[m, :, 5 * g + j].reshape(LV, MAIN)
                o_ref[m, r, :, :MAIN] = c_ref[m, r, :, :MAIN] + main
                tail = tails[:, TAIL * j : TAIL * (j + 1)]
                o_ref[m, r, :, MAIN:] = c_ref[m, r, :, MAIN:] + tail
            part = (m, pl.ds(4 * g, 4))
            n = len(stores)
            stores.append(pltpu.make_async_copy(o_ref.at[part], o_hbm.at[part], sems.at[n]))
            stores[-1].start()
    for copy in stores:
        copy.wait()


def finish(y, control):
    n = y.shape[0]
    shape = (n, ROWS, LV, NY)
    return pl.pallas_call(
        finish_body,
        in_specs=[HBM, WHOLE],
        out_specs=HBM,
        out_shape=pltpu.HBM(shape, f32),
        scratch_shapes=[
            pltpu.VMEM(y.shape, f32),
            pltpu.VMEM(shape, f32),
            dma((n * GROUPS,)),
            dma((n * GROUPS,)),
        ],
        compiler_params=params(16),
        name="finish",
    )(in_hbm(y), control)


def unpack_wind_body(me_ref, *refs):
    got_refs, o_ref, x_ref = refs[:MEMS], refs[MEMS], refs[MEMS + 1]
    for k in range(MEMS):
        x_ref[lax.rem(me_ref[0] + MEMS - k, MEMS)] = got_refs[k][...]
    for c in range(2):
        last = x_ref[0, c, FULL]
        for i in range(1, MEMS):
            last = jnp.where(own_cut(i, last.shape), x_ref[i, c, FULL], last)
        for r in range(ROWS):
            k = main_at(r)
            o_ref[c, r, :, :MAIN] = x_ref[k % MEMS, c, k // MEMS]
        for g in range(GROUPS):
            k = tail_at(g)
            tails = last if k == LAST else x_ref[k % MEMS, c, k // MEMS]
            for j in range(4):
                o_ref[c, 4 * g + j, :, MAIN:] = tails[:, TAIL * j : TAIL * (j + 1)]


def unpack_wind(me, got):
    return pl.pallas_call(
        unpack_wind_body,
        in_specs=[SMEM] + [WHOLE] * MEMS,
        out_shape=jax.ShapeDtypeStruct((2, ROWS, LV // MEMS, NY), f32),
        scratch_shapes=[pltpu.VMEM((MEMS, 2, Q, LV // MEMS, MAIN), f32)],
        compiler_params=params(8),
        name="unpack_wind",
    )(me, *got)


def spread_body(me_ref, x_hbm, *refs):
    o_refs, (x_ref, packed, in_sems, out_sems) = refs[:MEMS], refs[MEMS:]
    count = x_ref.shape[0]
    loads = [pltpu.make_async_copy(x_hbm.at[n], x_ref.at[n], in_sems.at[n]) for n in range(count)]
    for copy in loads:
        copy.start()
    stores = []
    for n in range(count):
        loads[n].wait()

        def keep(k, value):
            packed[n, k % MEMS, LV * (k // MEMS) : LV * (k // MEMS + 1)] = value

        for r in range(ROWS):
            keep(main_at(r), x_ref[n, r, :, :MAIN])
        for g in range(GROUPS):
            tails = jnp.concatenate([x_ref[n, 4 * g + j, :, MAIN:] for j in range(4)], axis=1)
            if tail_at(g) != LAST:
                keep(tail_at(g), tails)
        tiles = [tails[8 * u : 8 * (u + 1)] for u in range(LV // 8)]
        for d in range(MEMS):
            joined = pltpu.roll(tiles[0], CUT * (-d % MEMS), 1) if d else tiles[0]
            for u in range(1, LV // 8):
                shift = (u - d) % MEMS
                moved = pltpu.roll(tiles[u], CUT * shift, 1) if shift else tiles[u]
                joined = jnp.where(own_cut(u, joined.shape), moved, joined)
            packed[n, d, FULL * LV :] = joined
        for k in range(MEMS):
            share = packed.at[n, lax.rem(me_ref[0] + k, MEMS)]
            stores.append(pltpu.make_async_copy(share, o_refs[k].at[n], out_sems.at[n, k]))
            stores[-1].start()
    for copy in stores:
        copy.wait()


def spread(me, x):
    n = x.shape[0]
    return pl.pallas_call(
        spread_body,
        in_specs=[SMEM, HBM],
        out_specs=[HBM] * MEMS,
        out_shape=[pltpu.HBM((n, SHARE, MAIN), f32)] * MEMS,
        scratch_shapes=[
            pltpu.VMEM(x.shape, f32),
            pltpu.VMEM((n, MEMS, SHARE, MAIN), f32),
            dma((n,)),
            dma((n, MEMS)),
        ],
        compiler_params=params(16),
        name="spread",
    )(me, in_hbm(x))


def field_rows(k, f):
    return pl.ds(8 * k + f, TILES, stride=8 * K)


def share_rows(i, at):
    return pl.ds(i * TILES * K + at, TILES, stride=K)


def load_tile(ref, shared, k, f):
    if not shared:
        return ref[field_rows(k, f), :]
    return ref[share_rows(k % MEMS, 8 * (k // MEMS) + f), :]


def filter_body(
    out_shared, x_ref, w_ref, gy_ref, ga_ref, gb_ref, gc_ref, o_hbm, ra_ref, rb_ref, rc_ref, last_ref, tails_ref, s_ref, o_ref, sems,
):
    wide = 2 * MAIN
    if out_shared:
        for f in range(FIELDS):
            last_ref[f] = load_tile(x_ref, False, LAST, f)
    else:
        pieces = [x_ref[share_rows(i, 8 * FULL), :] for i in range(MEMS)]
        for f in range(FIELDS):
            last = None
            for i in range(MEMS):
                shift = (i - f) % MEMS
                moved = pltpu.roll(pieces[i], CUT * shift, 1) if shift else pieces[i]
                last = moved if i == 0 else jnp.where(own_cut(i, moved.shape), moved, last)
            last_ref[f] = last

    def keep(s, j, lanes, value):
        for n, part in enumerate(split(value)):
            if s == 0:
                first = min(SPAN * (j + 1), FIRST) - SPAN * j
                ra_ref[n, SPAN * j : SPAN * j + first, lanes] = part[:first]
                if first < SPAN:
                    rb_ref[n, 0, :REST, lanes] = part[first:]
                    rb_ref[n, 1, :REST, lanes] = part[first:]
            elif s == 1:
                at = REST + SPAN * (j // 2)
                rb_ref[n, j % 2, at : at + SPAN, lanes] = part
            else:
                rc_ref[n, j, residue(s - 2), lanes] = part

    def y_filter(pair):
        parts = []
        for f in pair:
            for j in range(4):
                for g in range(GROUPS):
                    k = tail_at(g)
                    tail = last_ref[f] if k == LAST else load_tile(x_ref, not out_shared, k, f)
                    if j:
                        tail = pltpu.roll(tail, MAIN - TAIL * j, 1)
                    tail = tail[:, :TAIL]
                    main = load_tile(x_ref, not out_shared, main_at(4 * g + j), f)
                    parts.append(jnp.concatenate([main, tail], axis=1))
        hi, lo = split(jnp.concatenate(parts, axis=0))
        rows, cols = hi.shape[0], NS * NY
        both = dot(jnp.concatenate([hi, lo], axis=0), gy_ref[:, : cols + MAIN])
        y = both[:rows, :cols] + both[rows:, :cols]
        other = dot(hi, gy_ref[:, cols + MAIN :])
        y = y + jnp.concatenate([other, both[:rows, cols:]], axis=1)
        for i, f in enumerate(pair):
            lanes = slice(MAIN * f, MAIN * (f + 1))
            for j in range(4):
                at = SPAN * (4 * i + j)
                part = y[at : at + SPAN] * w_ref[f : f + 1, :]
                for s in range(NS):
                    keep(s, j, lanes, part[:, MAIN * s : MAIN * (s + 1)])
                tails_ref[f, j] = part[:, NS * MAIN :]

    def keep_tails():
        for q in range(FIELDS // 4):
            lanes = slice(MAIN * (FIELDS + q), MAIN * (FIELDS + q + 1))
            for j in range(4):
                for s in range(NS):
                    lane = TAIL * s
                    parts = [tails_ref[4 * q + i, j, :, lane : lane + TAIL] for i in range(4)]
                    keep(s, j, lanes, jnp.concatenate(parts, axis=1))

    def x_filter(lanes):
        def product(g, hi, lo):
            rows = g.shape[0] // 2
            both = dot(g, hi)
            return both[:rows] + both[rows:] + dot(g[:rows], lo)

        a = product(ga_ref[...], ra_ref[0, :, lanes], ra_ref[1, :, lanes])
        b = [product(gb_ref[p], rb_ref[0, p, :, lanes], rb_ref[1, p, :, lanes]) for p in range(2)]
        c = [product(gc_ref[j], rc_ref[0, j, :, lanes], rc_ref[1, j, :, lanes]) for j in range(4)]
        return [a[residue(j)] + b[j % 2][residue(j // 2)] + c[j] for j in range(4)]

    def x_main(pair):
        out = x_filter(slice(MAIN * pair[0], MAIN * pair[0] + wide))
        for i, f in enumerate(pair):
            for r in range(ROWS):
                g, j = r // 4, r % 4
                main = out[j][TILES * g : TILES * (g + 1), MAIN * i : MAIN * (i + 1)]
                at = TILES * (K * f + main_at(r))
                s_ref[at : at + TILES, :] = main

    def x_tails():
        out = x_filter(slice(MAIN * FIELDS, MAIN * FIELDS + wide))
        for f in range(FIELDS):
            lane = TAIL * f
            for g in range(GROUPS):
                rows = slice(TILES * g, TILES * (g + 1))
                parts = [out[j][rows, lane : lane + TAIL] for j in range(4)]
                back = out_shared and tail_at(g) == LAST
                at = TILES * (K * (FIELDS - 1 - f if back else f) + tail_at(g))
                s_ref[at : at + TILES, :] = jnp.concatenate(parts, axis=1)

    couples = [(f, f + 1) for f in range(0, FIELDS, 2)]
    y_filter(couples[0])
    y_filter(couples[1])
    x_main(couples[0])
    y_filter(couples[2])
    x_main(couples[1])
    y_filter(couples[3])
    keep_tails()
    x_main(couples[2])
    x_tails()
    x_main(couples[3])
    size = o_ref.shape[0] // MEMS
    stores = []
    for n in range(MEMS):
        if out_shared:
            cells = [(t, n + MEMS * q, K * (n * TILES + t) + 8 * q) for q in range(FULL) for t in range(TILES)]
        else:
            cells = [(t, k, 8 * (K * t + k)) for t in (2 * n, 2 * n + 1) for k in range(K)]
        for t, k, at in cells:
            o_ref[at : at + 8, :] = s_ref[pl.ds(TILES * k + t, FIELDS, stride=TILES * K), :]
        for t in range(TILES if out_shared else 0):
            tile = s_ref[pl.ds(TILES * LAST + t, FIELDS, stride=TILES * K), :]
            at = K * (n * TILES + t) + 8 * FULL
            o_ref[at : at + 1, :] = gather_row(tile, CUT * (-n % MEMS))
        part = pl.ds(size * n, size)
        stores.append(pltpu.make_async_copy(o_ref.at[part], o_hbm.at[part], sems.at[n]))
        stores[-1].start()
    for copy in stores:
        copy.wait()


def filter_fields(x, w, filters, out_shared):
    rows = TILES * FIELDS * K
    columns = FIELDS * NY
    return pl.pallas_call(
        lambda *refs: filter_body(out_shared, *refs),
        in_specs=[WHOLE] * (2 + len(filters)),
        out_specs=HBM,
        out_shape=pltpu.HBM((rows, MAIN), f32),
        scratch_shapes=[
            pltpu.VMEM((2, FIRST, columns), bf16),
            pltpu.VMEM((2, 2, PAIR, columns), bf16),
            pltpu.VMEM((2, 4, 2 * SPAN, columns), bf16),
            pltpu.VMEM((FIELDS, TILES, MAIN), f32),
            pltpu.VMEM((FIELDS, 4, SPAN, MAIN), f32),
            pltpu.VMEM((FIELDS * K * TILES, MAIN), f32),
            pltpu.VMEM((rows, MAIN), f32),
            dma((MEMS,)),
        ],
        compiler_params=params(36),
        name="filter_out" if out_shared else "filter_back",
    )(x, w, *filters)


def mix(v, x):
    hi, lo = split(x)
    return dot(v[0], hi) + dot(v[0], lo) + dot(v[1], hi)


def middle_body(scale, me_ref, x_ref, v_ref, *refs):
    e_refs, o_ref, wind_refs = list(refs[:MEMS]), refs[MEMS], refs[MEMS + 1 : 2 * MEMS + 1]
    cut_ref, wind_ref, ens_ref, sems = refs[2 * MEMS + 1 :]
    loads = [pltpu.make_async_copy(e_refs[k], ens_ref.at[k], sems.at[k]) for k in range(MEMS)]
    for copy in loads:
        copy.start()
    e_refs = [ens_ref.at[k] for k in range(MEMS)]
    v, vt = split(v_ref[...]), split(v_ref[...].T)
    me = me_ref[0]
    wind = [None, None]
    for k in range(MEMS):
        loads[k].wait()
        at = lax.rem(me + MEMS - k, MEMS)
        for m in range(2):
            tiles = []
            for q in range(FULL):
                parts = [x_ref[at, m, K * u + 8 * q : K * u + 8 * (q + 1), :] for u in range(LV // 8)]
                tiles.append(jnp.concatenate(parts, axis=0))
            parts = []
            for u in range(LV // 8):
                row = x_ref[at, m, K * u + 8 * FULL : K * (u + 1), :]
                row = pltpu.roll(jnp.broadcast_to(row, (8, MAIN)), CUT * lax.rem(me + 1, MEMS), 1)
                parts.append(pltpu.roll(row, 0, 1, stride=CUT, stride_axis=0))
            tiles.append(jnp.concatenate(parts, axis=0))
            loc = mix(v, jnp.concatenate(tiles, axis=1))
            for c in range(2):
                joined = e_refs[k][m, c, FULL * LV :]
                for u in range(LV // 8):
                    moved = pltpu.roll(joined, CUT * lax.rem(me + MEMS - u, MEMS), 1)
                    cut_ref[k, m, c, 8 * u : 8 * (u + 1)] = moved
                tiles = [e_refs[k][m, c, LV * q : LV * (q + 1)] for q in range(FULL)]
                ens = jnp.concatenate(tiles + [cut_ref[k, m, c]], axis=1)
                wind[c] = ens * loc if wind[c] is None else wind[c] + ens * loc
    wind = [w * scale for w in wind]
    for c in range(2):
        for q in range(Q):
            tile = wind[c][:, MAIN * q : MAIN * (q + 1)]
            wind_ref[:, c, q] = tile.reshape(MEMS, LV // MEMS, MAIN)
    for k in range(MEMS):
        wind_refs[k][...] = wind_ref[lax.rem(me + k, MEMS)]
    for k in range(MEMS):
        at = lax.rem(me + MEMS - k, MEMS)
        for m in range(2):
            adj = None
            for c in range(2):
                tiles = [e_refs[k][m, c, LV * q : LV * (q + 1)] for q in range(FULL)]
                ens = jnp.concatenate(tiles + [cut_ref[k, m, c]], axis=1)
                adj = ens * wind[c] if adj is None else adj + ens * wind[c]
            back = mix(vt, adj * scale)
            for u in range(LV // 8):
                for q in range(FULL):
                    tile = back[8 * u : 8 * (u + 1), MAIN * q : MAIN * (q + 1)]
                    o_ref[at, m, K * u + 8 * q : K * u + 8 * (q + 1), :] = tile
                row = gather_row(back[8 * u : 8 * (u + 1), MAIN * FULL :], CUT * lax.rem(MEMS - me, MEMS))
                o_ref[at, m, K * u + 8 * FULL : K * (u + 1), :] = row


def middle(me, x, v, ens, scale):
    return pl.pallas_call(
        lambda *refs: middle_body(scale, *refs),
        in_specs=[SMEM, WHOLE, WHOLE] + [HBM] * MEMS,
        out_specs=[WHOLE] * (1 + MEMS),
        out_shape=[jax.ShapeDtypeStruct((MEMS, 2, LV // 8 * K, MAIN), f32)]
        + [jax.ShapeDtypeStruct((2, Q, LV // MEMS, MAIN), f32)] * MEMS,
        scratch_shapes=[
            pltpu.VMEM((MEMS, 2, 2, LV, MAIN), f32),
            pltpu.VMEM((MEMS, 2, Q, LV // MEMS, MAIN), f32),
            pltpu.VMEM((MEMS,) + ens[0].shape, f32),
            dma((MEMS,)),
        ],
        compiler_params=params(24),
        name="middle",
    )(me, x, v, *[in_hbm(e) for e in ens])


def swap(x, axes):
    return lax.all_to_all(x, axes, 0, 0, tiled=True)


ORDER = (2, 6, 4, 3, 5, 1, 7)


def shards(control, ens_perts, vert_corr, slab_wts, level_slab):
    members = control.shape[0]
    scale = 1.0 / math.sqrt(members * MEMS - 1)
    filters = constants()

    control = jnp.transpose(control, (0, 2, 1, 3))
    got = swap(pack(control).reshape(TILES, K, FIELDS, MAIN), "tile")

    me = lax.axis_index("mem").reshape(1)
    ens = jnp.transpose(ens_perts, (0, 1, 3, 2, 4)).reshape(4, ROWS, LV, NY)
    ens = list(spread(me, ens))
    for k in ORDER:
        ens[k] = lax.ppermute(ens[k], "mem", [(i, (i + k) % MEMS) for i in range(MEMS)])
    ens = [e.reshape(2, 2, SHARE, MAIN) for e in ens]

    level_wts = slab_wts[level_slab]
    first = FIELDS * (lax.axis_index("tile") % (LV // FIELDS))
    own = lax.dynamic_slice_in_dim(level_wts, first, FIELDS, 0)
    w = jnp.concatenate([jnp.repeat(own, MAIN, axis=1), jnp.repeat(own, TAIL, axis=1)], axis=1)

    smooth = filter_fields(got.reshape(TILES * K * FIELDS, MAIN), w, filters, True)
    got = swap(smooth.reshape(MEMS * TILES * K, 1, MAIN), ("mem", "tile"))
    got = got.reshape(MEMS, 2, LV // 8 * K, MAIN)
    adj, *wind = middle(me, got, vert_corr, ens, scale)
    got = swap(adj.reshape(MEMS * TILES * K, 1, MAIN), ("mem", "tile"))
    smooth = filter_fields(got.reshape(MEMS * TILES * K, MAIN), w, filters, False)
    smooth, wind = lax.optimization_barrier((smooth, wind))
    got = swap(smooth.reshape(TILES, K, FIELDS, MAIN), "tile")
    for k in range(1, MEMS):
        wind[k] = lax.ppermute(wind[k], "mem", [(i, (i + k) % MEMS) for i in range(MEMS)])
    wind = unpack_wind(me, wind)
    gradient = finish(got.reshape(2, LV // 8, K, 8, MAIN), control)
    return (jnp.transpose(wind, (0, 2, 1, 3)), jnp.transpose(gradient, (0, 2, 1, 3)))


def solution(mesh):
    return jax.shard_map(
        shards,
        mesh=mesh,
        in_specs=(P("mem", None, "tile", None), P("mem", None, None, "tile", None), P(), P(), P()),
        out_specs=(P(None, "mem", "tile", None), P("mem", None, "tile", None)),
        check_vma=False,
    )
```
